32 devices in a mesh: atoms: 8 (over z, y), space: 4 (over x, core).
Axes of the slice: x: 2, y: 2, z: 4, core: 2. Of those that a mesh axis runs over, the one named last changes fastest.
Arguments:
- block_store: bfloat16 [4, 32, 128, 128], P('space', 'atoms'), may hold values from -0.21875 to 0.21875
- block_source: int32 [8, 4, 36], P('atoms', 'space'), may hold values from 0 to 31, as said below
- chem_pot: float32 [1], replicated, may hold values from -0.6 to 0.6
- basis_values: bfloat16 [8, 4, 8, 128, 1024], P('atoms', 'space'), may hold values from -1.5 to 1.5
- core_density: float32 [8, 4, 1024], P('atoms', 'space'), may hold values from 0.5 to 4
- point_weights: float32 [8, 4, 1024], P('atoms', 'space'), may hold values from 0.2 to 0.8
- pair_dest: int32 [8, 4, 12], P('atoms', 'space'), may hold values from 0 to 3, as said below
- tile_pairs: int32 [8, 4, 2, 12], P('atoms', 'space'), may hold values from -1 to 7, as said below
Outputs:
- density: bfloat16 [8, 4, 768, 128], P('atoms', 'space')
- potential: float32 [8, 4, 1024], P('atoms', 'space')
- kohn_sham: float32 [8, 4, 768, 128], P('atoms', 'space')
The draws below stay inside these ranges and needn't reach their ends.
Inputs may be any that keep to these rules, and one draw needn't show every extreme that they name: `block_source`: each device names at most 5 blocks whose number // 4 is the same; blocks may repeat. `pair_dest`: the two pairs of one density block go to different tiles; a device sends at most 3 pairs to one tile. `tile_pairs`: slots that receive no pair hold -1 in both entries; the others follow the pairs as stated.
All inputs are finite; a program needn't handle non-finite values.
Results may differ from the reference program's by a relative error of at most 0.0065.
Values may be sent and summed in bfloat16 or wider, within the bound.
No kernel may reach another device: no remote copies, remote signals or barrier semaphores. Data moves between devices by JAX's collectives and lax.ppermute only.
A program may use at most 64 MiB of HBM per device.

```python
import math
import jax
import jax.numpy as jnp
from jax import lax

B = 128
KB = 6
M = 768
SLOTS = 36
SENDS = 12
NB_DEV = 4
NLOC = 8
PTS = 1024
CAPT = 3
N_ATOMS = 8
N_SPACE = 4


def draw_block_source(key, part):
    device_keys = jax.random.split(key, N_ATOMS * N_SPACE)
    atom_ids = jnp.arange(N_ATOMS * N_SPACE) // N_SPACE

    def single(one_key, atom_id):
        first_key, second_key = jax.random.split(one_key)
        shuffled = jax.random.permutation(first_key, N_ATOMS).astype(jnp.int32)
        target = jnp.where(atom_id == 0, N_ATOMS - 1, jnp.where(atom_id == N_ATOMS - 1, 0, shuffled[0]))
        swapped = jnp.where(shuffled == target, shuffled[0], shuffled)
        swapped = swapped.at[0].set(target)
        peers = swapped[jnp.arange(SLOTS) % N_ATOMS]
        chosen = jax.random.randint(second_key, (SLOTS,), 0, NB_DEV)
        forced = jnp.where(atom_id == 0, NB_DEV - 1, jnp.where(atom_id == N_ATOMS - 1, 0, chosen[0]))
        chosen = chosen.at[0].set(forced)
        return (peers * NB_DEV + chosen).astype(jnp.int32)
    return jax.vmap(single)(device_keys, atom_ids).reshape(N_ATOMS, N_SPACE, SLOTS)


def pair_tables(key):
    base_key = jax.random.fold_in(key, 811)

    def group(atom_id):
        group_key = jax.random.fold_in(base_key, atom_id)
        order_keys = jax.random.split(jax.random.fold_in(group_key, 1), N_SPACE)
        orders = jax.vmap(lambda one_key: jax.random.permutation(one_key, N_SPACE))(order_keys).astype(jnp.int32)
        sends = jnp.arange(SENDS)
        destinations = orders[:, sends % N_SPACE]
        arrival = sends // N_SPACE
        row_blocks = jax.random.randint(jax.random.fold_in(group_key, 2), (N_SPACE, SENDS), 0, NLOC)
        col_blocks = jax.random.randint(jax.random.fold_in(group_key, 3), (N_SPACE, SENDS), 0, NLOC)
        row_blocks = row_blocks.at[0, 0].set(jnp.where(atom_id == 0, NLOC - 1, row_blocks[0, 0]))
        slot_at = jnp.arange(N_SPACE)[:, None] * CAPT + arrival[None, :]
        table = jnp.full((N_SPACE, 2, N_SPACE * CAPT), -1, jnp.int32)
        table = table.at[destinations, 0, slot_at].set(row_blocks.astype(jnp.int32))
        table = table.at[destinations, 1, slot_at].set(col_blocks.astype(jnp.int32))
        return (destinations.astype(jnp.int32), table)
    return jax.vmap(group)(jnp.arange(N_ATOMS))


def draw_pair_dest(key, part):
    return pair_tables(key)[0]


def draw_tile_pairs(key, part):
    return pair_tables(key)[1]


def block_levels(own_key, shape, pieces, least, high):
    level = 1.0
    for dim, blocks in pieces:
        heights = jax.random.uniform(jax.random.fold_in(jax.random.fold_in(own_key, 6), dim), (blocks,), jnp.float32, least / len(pieces), high / len(pieces))
        level = level * jnp.repeat(jnp.exp(heights), shape[dim] // blocks).reshape((-1,) + (1,) * (len(shape) - 1 - dim))
    return level


def noise(key, extent, spread, most, cuts=(), kind=jnp.bfloat16):
    loudness = block_levels(key, extent, cuts, -0.22, 0.18) if cuts else 1.0
    values = jax.random.normal(key, extent, jnp.float32) * spread * loudness
    return jnp.minimum(jnp.maximum(values, -most), most).astype(kind)


def setup_inputs(seed: int = 0) -> dict:
    splits = jax.random.split(jax.random.key(seed), 9)
    block_store = noise(splits[0], (N_SPACE, N_ATOMS * NB_DEV, B, B), M ** -0.5, 0.21875, ((0, 4), (1, 8)))
    block_source = draw_block_source(jax.random.fold_in(splits[8], 71), 0)
    chem_pot = jnp.clip(jax.random.uniform(splits[2], (1,), jnp.float32, -0.6, 0.6), -0.6, 0.6)
    basis_values = noise(splits[3], (N_ATOMS, N_SPACE, NLOC, B, PTS), 0.25, 1.5, ((0, 8), (1, 4)))
    core_density = jnp.clip(jnp.exp(math.log(4.0) - 2.0794415 * jax.random.uniform(splits[4], (N_ATOMS, N_SPACE, PTS), jnp.float32) ** block_levels(splits[4], (N_ATOMS, N_SPACE, PTS), ((0, 8), (1, 4)), -0.2, 0.2)), 0.5, 4.0)
    point_weights = jnp.clip(0.2 + 0.6 * jax.random.uniform(splits[5], (N_ATOMS, N_SPACE, PTS), jnp.float32) ** block_levels(splits[5], (N_ATOMS, N_SPACE, PTS), ((0, 8), (1, 4)), -0.2, 0.2), 0.2, 0.8)
    pair_dest = draw_pair_dest(jax.random.fold_in(splits[8], 71), 0)
    tile_pairs = draw_tile_pairs(jax.random.fold_in(splits[8], 71), 0)
    return {"block_store": block_store, "block_source": block_source, "chem_pot": chem_pot, "basis_values": basis_values, "core_density": core_density, "point_weights": point_weights, "pair_dest": pair_dest, "tile_pairs": tile_pairs}


slater_factor = math.pow(3.0 / math.pi, 1.0 / 3.0)
density_floor = 0.05

def sign_density(blocks, chem):
    matrix = blocks.reshape(KB, KB, B, B).transpose(0, 2, 1, 3).reshape(M, M)
    widened = matrix.astype(jnp.float32)
    identity = jnp.eye(M, dtype=jnp.float32)
    shifted = 0.5 * (widened + widened.T) - chem * identity
    scaling = 2.0 * jnp.sqrt(jnp.sum(shifted * shifted) / M + 1e-06)
    start_x = (shifted / scaling).astype(jnp.bfloat16)
    square_one = jnp.dot(start_x, start_x, preferred_element_type=jnp.float32)
    factor_one = (1.5 * identity - 0.5 * square_one).astype(jnp.bfloat16)
    next_x = jnp.dot(start_x, factor_one, preferred_element_type=jnp.float32).astype(jnp.bfloat16)
    square_two = jnp.dot(next_x, next_x[:, :B], preferred_element_type=jnp.float32)
    factor_two = (1.5 * identity[:, :B] - 0.5 * square_two).astype(jnp.bfloat16)
    final_x = jnp.dot(next_x, factor_two, preferred_element_type=jnp.float32)
    return (0.5 * (identity[:, :B] - final_x)).astype(jnp.bfloat16)

def reference(block_store, block_source, chem_pot, basis_values, core_density, point_weights, pair_dest, tile_pairs):
    chem = chem_pot[0]
    flat_source = block_source.reshape(N_ATOMS * N_SPACE, SLOTS)
    space_index = (jnp.arange(N_ATOMS * N_SPACE) % N_SPACE).astype(jnp.int32)

    def one_device(items):
        source, space_at = items
        row_store = jnp.take(block_store, space_at, axis=0)
        blocks = jnp.take(row_store, source, axis=0)
        return sign_density(blocks, chem)
    density = lax.map(one_device, (flat_source, space_index)).reshape(N_ATOMS, N_SPACE, M, B)

    def tile_group(items):
        columns, tables, cores, weights, destinations, slot_tables = items
        order = jnp.arange(SENDS)
        earlier = (destinations[:, :, None] == destinations[:, None, :]) & (order[None, None, :] < order[None, :, None])
        arrival = lax.optimization_barrier(jnp.sum(earlier.astype(jnp.int32), axis=2)).astype(jnp.int32)
        slot_at = (jnp.arange(N_SPACE)[:, None] * CAPT + arrival).astype(jnp.int32)
        row_blocks = slot_tables[destinations, 0, slot_at].reshape(-1)
        col_blocks = slot_tables[destinations, 1, slot_at].reshape(-1)
        dest_flat = destinations.reshape(-1)
        left_basis = tables[dest_flat, row_blocks].astype(jnp.float32)
        right_basis = tables[dest_flat, col_blocks].astype(jnp.float32)
        pair_blocks = columns.reshape(N_SPACE, KB, B, B)[:, order // 2].reshape(-1, B, B)
        product = jnp.einsum('nij,njp->nip', pair_blocks.astype(jnp.float32), right_basis)
        terms = lax.optimization_barrier(jnp.sum(left_basis * product, axis=1))
        valence = jnp.zeros((N_SPACE, PTS), jnp.float32).at[dest_flat].add(terms)
        potential = -slater_factor * jnp.cbrt(jnp.maximum(cores + valence, density_floor))
        scaled = weights * potential
        weighted = (left_basis * scaled[dest_flat][:, None, :]).astype(jnp.bfloat16)
        partial_value = jnp.einsum('nip,njp->nij', weighted.astype(jnp.float32), right_basis).astype(jnp.bfloat16)
        kohn = partial_value.astype(jnp.float32).reshape(N_SPACE, KB, 2, B, B).sum(axis=2).reshape(N_SPACE, M, B)
        return (potential, kohn)
    potential, kohn_sham = lax.map(tile_group, (density, basis_values, core_density, point_weights, pair_dest, tile_pairs))
    return (density, potential, kohn_sham)
```

```python
import functools
import math

import jax
import jax.numpy as jnp
from jax import lax
from jax.experimental import pallas as pl
from jax.experimental.pallas import tpu as pltpu
from jax.sharding import PartitionSpec as P

KB = 6


slater_factor = math.pow(3.0 / math.pi, 1.0 / 3.0)
density_floor = 0.05

VMEM = pl.BlockSpec(memory_space=pltpu.VMEM)
SMEM = pl.BlockSpec(memory_space=pltpu.SMEM)


def earlier_count(labels):
    order = jnp.arange(labels.shape[0])
    earlier = (labels[None, :] == labels[:, None]) & (order[None, :] < order[:, None])
    return jnp.sum(earlier.astype(jnp.int32), axis=1)


def requested_blocks(stored, source):
    held_count, block_width, _ = stored.shape
    atom_devices = lax.axis_size("atoms")
    capacity = pl.cdiv(source.shape[0], atom_devices)
    peer_index = source // held_count
    local_index = source % held_count
    slot_index = peer_index * capacity + earlier_count(peer_index)
    wanted = jnp.full((atom_devices * capacity,), -1, jnp.int32).at[slot_index].set(local_index)
    requested = lax.all_to_all(
        wanted.reshape(atom_devices, capacity), "atoms", split_axis=0, concat_axis=0, tiled=True
    )
    flat_request = requested.reshape(-1)
    chosen = jnp.take(stored, jnp.clip(flat_request, 0, held_count - 1), axis=0)
    arrived = lax.all_to_all(
        chosen.reshape(atom_devices, capacity, block_width, block_width),
        "atoms",
        split_axis=0,
        concat_axis=0,
        tiled=True,
    )
    return arrived.reshape(atom_devices * capacity, block_width, block_width), slot_index


def gathered_blocks(stored, source):
    held_count, block_width, _ = stored.shape
    atom_devices = lax.axis_size("atoms")
    inner = 2 if atom_devices % 2 == 0 else 1
    outer = atom_devices // inner
    me = lax.axis_index("atoms")
    columns = [stored]
    for step in range(1, outer):
        pairs = [(i, (i + step * inner) % atom_devices) for i in range(atom_devices)]
        columns.append(lax.ppermute(stored, "atoms", pairs))
    parts = list(columns)
    if inner == 2:
        flip = [(i, i ^ 1) for i in range(atom_devices)]
        parts += [lax.ppermute(part, "atoms", flip) for part in columns]
    peer = source // held_count
    step = (me // inner - peer // inner) % outer
    other = (me % inner) ^ (peer % inner)
    place = (other * outer + step) * held_count + source % held_count
    return jnp.concatenate(parts, axis=0), place


def partner(me, step, devices):
    if devices & (devices - 1) == 0:
        return me ^ abs(step)
    return (me + step) % devices


def step_to(me, other, devices):
    if devices & (devices - 1) == 0:
        return me ^ other
    return lax.rem(other - me + devices, devices)


def step_from(me, other, devices):
    if devices & (devices - 1) == 0:
        return me ^ other
    return lax.rem(me - other + devices, devices)


def exchange(groups, sign):
    devices = lax.axis_size("space")
    got = [groups[0]] + [None] * (devices - 1)
    for step in reversed(range(1, devices)):
        pairs = [(i, partner(i, sign * step, devices)) for i in range(devices)]
        got[step] = lax.ppermute(groups[step], "space", pairs)
    return got


def pair_places(dest_ref, me, devices, capacity):
    sends = dest_ref.shape[0]
    dests = [dest_ref[j] for j in range(sends)]
    places = []
    for j in range(sends):
        rank = jnp.int32(0)
        for earlier in range(j):
            rank += jnp.where(dests[earlier] == dests[j], 1, 0)
        places.append(step_to(me, dests[j], devices) * capacity + rank)
    return places


def sign_kernel(
    devices, capacity, place_ref, chem_ref, dest_ref, me_ref, block_ref, density_ref, *rest
):
    out_refs = rest[:devices]
    shifted, x_zero, t_one, x_one, pairs = rest[devices:]
    width = block_ref.shape[-1]
    order = KB * width
    rows = lax.broadcasted_iota(jnp.int32, (width, width), 0)
    cols = lax.broadcasted_iota(jnp.int32, (width, width), 1)
    diagonal = rows == cols
    unit = jnp.where(diagonal, 1.0, 0.0)
    chem = chem_ref[0]

    def at(i):
        return pl.ds(i * width, width)

    total = jnp.zeros((8, width), jnp.float32)
    tiles = [(i, j) for i in range(KB) for j in range(i, KB)]
    for i, j in tiles:
        upper = block_ref[place_ref[i * KB + j]].astype(jnp.float32)
        lower = block_ref[place_ref[j * KB + i]].astype(jnp.float32)
        value = 0.5 * (upper + lower.T)
        if i == j:
            value = value - chem * unit
        shifted[at(i), at(j)] = value
        squares = (value * value).reshape(width // 8, 8, width).sum(axis=0)
        total = total + (squares if i == j else 2.0 * squares)
    mean = jnp.sum(total, keepdims=True) / order
    inverse = 1.0 / (2.0 * jnp.sqrt(mean + 1e-06))
    for i, j in tiles:
        value = (shifted[at(i), at(j)] * inverse).astype(jnp.bfloat16)
        x_zero[at(i), at(j)] = value
        if i != j:
            x_zero[at(j), at(i)] = value.T
    for i in range(KB):
        square = jnp.dot(x_zero[at(i), :], x_zero[...], preferred_element_type=jnp.float32)
        for j in range(KB):
            part = -0.5 * square[:, j * width : (j + 1) * width]
            t_one[at(i), at(j)] = (1.5 * unit + part if i == j else part).astype(jnp.bfloat16)
    for i in range(KB):
        x_one[at(i), :] = jnp.dot(
            x_zero[at(i), :], t_one[...], preferred_element_type=jnp.float32
        ).astype(jnp.bfloat16)
    square = jnp.dot(x_one[...], x_one[:, at(0)], preferred_element_type=jnp.float32)
    parts = []
    for i in range(KB):
        part = -0.5 * square[i * width : (i + 1) * width]
        parts.append((1.5 * unit + part if i == 0 else part).astype(jnp.bfloat16))
    t_two = jnp.concatenate(parts, axis=0)
    final = jnp.dot(x_one[...], t_two, preferred_element_type=jnp.float32)
    for i in range(KB):
        part = final[i * width : (i + 1) * width]
        density_ref[at(i), :] = (0.5 * (unit - part if i == 0 else -part)).astype(jnp.bfloat16)
    places = pair_places(dest_ref, me_ref[0], devices, capacity)
    for j, place in enumerate(places):
        pairs[place] = density_ref[at(j // 2), :]
    for k in range(devices):
        out_refs[k][...] = pairs[k * capacity : (k + 1) * capacity]


def grid_kernel(devices, capacity, full, me_ref, pick_ref, table_ref, core_ref, weight_ref, *rest):
    in_refs = rest[:devices]
    potential_ref = rest[devices]
    out_refs = rest[devices + 1 :]
    points = table_ref.shape[-1]
    width = table_ref.shape[1]
    me = me_ref[0]
    slots = []
    for k in range(devices):
        owner = step_from(me, k, devices)
        for c in range(capacity):
            slot = owner * capacity + c
            slots.append((k, c, pick_ref[0, slot], pick_ref[1, slot]))
    total = jnp.zeros((8, points), jnp.float32)
    for k, c, u, v in slots:
        left = table_ref[jnp.maximum(u, 0)].astype(jnp.float32)
        right = table_ref[jnp.maximum(v, 0)]
        product = jnp.dot(in_refs[k][c], right, preferred_element_type=jnp.float32)
        term = (left * product).reshape(width // 8, 8, points).sum(axis=0)
        total = total + term if full else jnp.where(u >= 0, total + term, total)
    valence = jnp.sum(total, axis=0, keepdims=True)
    value = jnp.maximum(core_ref[...] + valence, density_floor)
    root = jnp.exp(jnp.log(value) * (1.0 / 3.0))
    root = root - (root * root * root - value) / (3.0 * root * root)
    potential = -slater_factor * root
    potential_ref[...] = potential
    scaled = weight_ref[...] * potential
    for k, c, u, v in slots:
        left = table_ref[jnp.maximum(u, 0)].astype(jnp.float32)
        right = table_ref[jnp.maximum(v, 0)]
        weighted = (left * scaled).astype(jnp.bfloat16)
        out_refs[k][c] = lax.dot_general(
            weighted, right, (((1,), (1,)), ((), ())), preferred_element_type=jnp.float32
        ).astype(jnp.bfloat16)


def sum_kernel(devices, capacity, dest_ref, me_ref, *rest):
    in_refs = rest[:devices]
    kohn_ref, pairs = rest[devices:]
    width = kohn_ref.shape[-1]
    for k in range(devices):
        pairs[k * capacity : (k + 1) * capacity] = in_refs[k][...]
    places = pair_places(dest_ref, me_ref[0], devices, capacity)
    for i in range(KB):
        kohn_ref[pl.ds(i * width, width), :] = pairs[places[2 * i]].astype(jnp.float32) + pairs[
            places[2 * i + 1]
        ].astype(jnp.float32)


def per_device(
    block_store,
    block_source,
    chem_pot,
    basis_values,
    core_density,
    point_weights,
    pair_dest,
    tile_pairs,
):
    stored = block_store[0]
    held_count, block_width, _ = stored.shape
    source = block_source[0, 0]
    atom_devices = lax.axis_size("atoms")
    devices = lax.axis_size("space")
    if pl.cdiv(source.shape[0], atom_devices) < held_count:
        blocks, place = requested_blocks(stored, source)
    else:
        blocks, place = gathered_blocks(stored, source)
    destinations = pair_dest[0, 0]
    send_count = destinations.shape[0]
    capacity = pl.cdiv(send_count, devices)
    order = KB * block_width
    me = lax.axis_index("space").reshape(1)
    group = jax.ShapeDtypeStruct((capacity, block_width, block_width), jnp.bfloat16)
    out = pl.pallas_call(
        functools.partial(sign_kernel, devices, capacity),
        name="sign",
        in_specs=[SMEM] * 4 + [VMEM],
        out_shape=[jax.ShapeDtypeStruct((order, block_width), jnp.bfloat16)] + [group] * devices,
        out_specs=[VMEM] * (1 + devices),
        scratch_shapes=[
            pltpu.VMEM((order, order), jnp.float32),
            pltpu.VMEM((order, order), jnp.bfloat16),
            pltpu.VMEM((order, order), jnp.bfloat16),
            pltpu.VMEM((order, order), jnp.bfloat16),
            pltpu.VMEM((devices * capacity, block_width, block_width), jnp.bfloat16),
        ],
        compiler_params=pltpu.CompilerParams(vmem_limit_bytes=16 << 20),
        cost_estimate=pl.CostEstimate(
            flops=4 * order**3, bytes_accessed=4 * order * order, transcendentals=0
        ),
    )(place, chem_pot, destinations, me, blocks)
    density, outgoing = out[0], out[1:]
    incoming = exchange(outgoing, 1)
    tables = basis_values[0, 0]
    points = tables.shape[-1]
    out = pl.pallas_call(
        functools.partial(grid_kernel, devices, capacity, devices * capacity == send_count),
        name="grid",
        in_specs=[SMEM] * 2 + [VMEM] * (3 + devices),
        out_shape=[jax.ShapeDtypeStruct((1, points), jnp.float32)] + [group] * devices,
        out_specs=[VMEM] * (1 + devices),
        compiler_params=pltpu.CompilerParams(vmem_limit_bytes=24 << 20),
        cost_estimate=pl.CostEstimate(
            flops=4 * devices * capacity * block_width**2 * points,
            bytes_accessed=2 * tables.size,
            transcendentals=2 * points,
        ),
    )(me, tile_pairs[0, 0], tables, core_density[0], point_weights[0], *incoming)
    potential, partials = out[0], out[1:]
    returned = exchange(partials, -1)
    kohn = pl.pallas_call(
        functools.partial(sum_kernel, devices, capacity),
        name="sum",
        in_specs=[SMEM] * 2 + [VMEM] * devices,
        out_shape=jax.ShapeDtypeStruct((order, block_width), jnp.float32),
        out_specs=VMEM,
        scratch_shapes=[
            pltpu.VMEM((devices * capacity, block_width, block_width), jnp.bfloat16),
        ],
        compiler_params=pltpu.CompilerParams(vmem_limit_bytes=8 << 20),
    )(destinations, me, *returned)
    return (density[None, None], potential[None], kohn[None, None])


def solution(mesh):
    placed = (
        P("space", "atoms", None, None),
        P("atoms", "space", None),
        P(),
        P("atoms", "space", None, None, None),
        P("atoms", "space", None),
        P("atoms", "space", None),
        P("atoms", "space", None),
        P("atoms", "space", None, None),
    )
    return jax.shard_map(
        per_device,
        mesh=mesh,
        in_specs=placed,
        out_specs=(
            P("atoms", "space", None, None),
            P("atoms", "space", None),
            P("atoms", "space", None, None),
        ),
        check_vma=False,
    )
```

```python
import functools
import math

import jax
import jax.numpy as jnp
from jax import lax
from jax.experimental import pallas as pl
from jax.experimental.pallas import tpu as pltpu
from jax.sharding import PartitionSpec as P

KB = 6


slater_factor = math.pow(3.0 / math.pi, 1.0 / 3.0)
density_floor = 0.05

VMEM = pl.BlockSpec(memory_space=pltpu.VMEM)
SMEM = pl.BlockSpec(memory_space=pltpu.SMEM)


def earlier_count(labels):
    order = jnp.arange(labels.shape[0])
    earlier = (labels[None, :] == labels[:, None]) & (order[None, :] < order[:, None])
    return jnp.sum(earlier.astype(jnp.int32), axis=1)


def requested_blocks(stored, source):
    held_count, block_width, _ = stored.shape
    atom_devices = lax.axis_size("atoms")
    capacity = pl.cdiv(source.shape[0], atom_devices)
    peer_index = source // held_count
    local_index = source % held_count
    slot_index = peer_index * capacity + earlier_count(peer_index)
    wanted = jnp.full((atom_devices * capacity,), -1, jnp.int32).at[slot_index].set(local_index)
    requested = lax.all_to_all(
        wanted.reshape(atom_devices, capacity), "atoms", split_axis=0, concat_axis=0, tiled=True
    )
    flat_request = requested.reshape(-1)
    chosen = jnp.take(stored, jnp.clip(flat_request, 0, held_count - 1), axis=0)
    arrived = lax.all_to_all(
        chosen.reshape(atom_devices, capacity, block_width, block_width),
        "atoms",
        split_axis=0,
        concat_axis=0,
        tiled=True,
    )
    return arrived.reshape(atom_devices * capacity, block_width, block_width), slot_index


def gathered_blocks(stored, source):
    held_count, _, _ = stored.shape
    atom_devices = lax.axis_size("atoms")
    if atom_devices & (atom_devices - 1):
        return lax.all_gather(stored, "atoms", axis=0, tiled=True), source
    parts = [stored] + [None] * (atom_devices - 1)
    for offset in sorted(range(1, atom_devices), key=lambda r: (r.bit_count(), -r)):
        step = 2 if offset == 3 else offset & -offset
        pairs = [(i, i ^ step) for i in range(atom_devices)]
        parts[offset] = lax.ppermute(parts[offset ^ step], "atoms", pairs)
    me = lax.axis_index("atoms")
    place = (me ^ (source // held_count)) * held_count + source % held_count
    return jnp.concatenate(parts, axis=0), place


def partner(me, step, devices):
    if devices & (devices - 1) == 0:
        return me ^ abs(step)
    return (me + step) % devices


def step_to(me, other, devices):
    if devices & (devices - 1) == 0:
        return me ^ other
    return lax.rem(other - me + devices, devices)


def step_from(me, other, devices):
    if devices & (devices - 1) == 0:
        return me ^ other
    return lax.rem(me - other + devices, devices)


def exchange(groups, sign):
    devices = lax.axis_size("space")
    got = {}
    for step in sorted(groups, reverse=True):
        pairs = [(i, partner(i, sign * step, devices)) for i in range(devices)]
        got[step] = lax.ppermute(groups[step], "space", pairs) if step else groups[step]
    return got


def pair_places(dest_ref, me, devices, capacity):
    sends = dest_ref.shape[0]
    dests = [dest_ref[j] for j in range(sends)]
    places = []
    for j in range(sends):
        rank = jnp.int32(0)
        for earlier in range(j):
            rank += jnp.where(dests[earlier] == dests[j], 1, 0)
        places.append(step_to(me, dests[j], devices) * capacity + rank)
    return places


def sign_kernel(
    devices, capacity, place_ref, chem_ref, dest_ref, me_ref, block_ref, density_ref, *rest
):
    out_refs = rest[:devices]
    shifted, x_zero, t_one, x_one, pairs = rest[devices:]
    width = block_ref.shape[-1]
    order = KB * width
    rows = lax.broadcasted_iota(jnp.int32, (width, width), 0)
    cols = lax.broadcasted_iota(jnp.int32, (width, width), 1)
    diagonal = rows == cols
    unit = jnp.where(diagonal, 1.0, 0.0)
    chem = chem_ref[0]

    def at(i):
        return pl.ds(i * width, width)

    total = jnp.zeros((8, width), jnp.float32)
    tiles = [(i, j) for i in range(KB) for j in range(i, KB)]
    for i, j in tiles:
        upper = block_ref[place_ref[i * KB + j]].astype(jnp.float32)
        lower = block_ref[place_ref[j * KB + i]].astype(jnp.float32)
        value = 0.5 * (upper + lower.T)
        if i == j:
            value = value - chem * unit
        shifted[at(i), at(j)] = value
        squares = (value * value).reshape(width // 8, 8, width).sum(axis=0)
        total = total + (squares if i == j else 2.0 * squares)
    mean = jnp.sum(total, keepdims=True) / order
    inverse = 1.0 / (2.0 * jnp.sqrt(mean + 1e-06))
    for i, j in tiles:
        value = (shifted[at(i), at(j)] * inverse).astype(jnp.bfloat16)
        x_zero[at(i), at(j)] = value
        if i != j:
            x_zero[at(j), at(i)] = value.T
    for i in range(KB):
        square = jnp.dot(x_zero[at(i), :], x_zero[...], preferred_element_type=jnp.float32)
        for j in range(KB):
            part = -0.5 * square[:, j * width : (j + 1) * width]
            t_one[at(i), at(j)] = (1.5 * unit + part if i == j else part).astype(jnp.bfloat16)
    for i in range(KB):
        x_one[at(i), :] = jnp.dot(
            x_zero[at(i), :], t_one[...], preferred_element_type=jnp.float32
        ).astype(jnp.bfloat16)
    square = jnp.dot(x_one[...], x_one[:, at(0)], preferred_element_type=jnp.float32)
    parts = []
    for i in range(KB):
        part = -0.5 * square[i * width : (i + 1) * width]
        parts.append((1.5 * unit + part if i == 0 else part).astype(jnp.bfloat16))
    t_two = jnp.concatenate(parts, axis=0)
    final = jnp.dot(x_one[...], t_two, preferred_element_type=jnp.float32)
    for i in range(KB):
        part = final[i * width : (i + 1) * width]
        density_ref[at(i), :] = (0.5 * (unit - part if i == 0 else -part)).astype(jnp.bfloat16)
    places = pair_places(dest_ref, me_ref[0], devices, capacity)
    for j, place in enumerate(places):
        pairs[place] = density_ref[at(j // 2), :]
    for k in range(devices):
        out_refs[k][...] = pairs[k * capacity : (k + 1) * capacity]


def tile_slots(pick_ref, me, steps, devices, capacity):
    slots = []
    for k in steps:
        owner = step_from(me, k, devices)
        for c in range(capacity):
            slot = owner * capacity + c
            slots.append((k, c, pick_ref[0, slot], pick_ref[1, slot]))
    return slots


def pair_density(slots, total, full, table_ref, group_refs):
    width, points = table_ref.shape[1:]
    for k, c, u, v in slots:
        left = table_ref[jnp.maximum(u, 0)].astype(jnp.float32)
        right = table_ref[jnp.maximum(v, 0)]
        product = jnp.dot(group_refs[k][c], right, preferred_element_type=jnp.float32)
        term = (left * product).reshape(width // 8, 8, points).sum(axis=0)
        total = total + term if full else jnp.where(u >= 0, total + term, total)
    return total


def pair_partials(slots, scaled, table_ref, group_refs):
    for k, c, u, v in slots:
        left = table_ref[jnp.maximum(u, 0)].astype(jnp.float32)
        right = table_ref[jnp.maximum(v, 0)]
        weighted = (left * scaled).astype(jnp.bfloat16)
        group_refs[k][c] = lax.dot_general(
            weighted, right, (((1,), (1,)), ((), ())), preferred_element_type=jnp.float32
        ).astype(jnp.bfloat16)


def near_density_kernel(
    devices, capacity, full, steps, me_ref, pick_ref, table_ref, column_ref, *rest
):
    groups = dict(zip(steps, rest[: len(steps)]))
    total_ref, density_ref = rest[len(steps) :]
    density_ref[...] = column_ref[...]
    slots = tile_slots(pick_ref, me_ref[0], steps, devices, capacity)
    total = jnp.zeros(total_ref.shape, jnp.float32)
    total_ref[...] = pair_density(slots, total, full, table_ref, groups)


def far_kernel(
    devices, capacity, full, steps, me_ref, pick_ref, table_ref, core_ref, weight_ref, near_ref, *rest
):
    groups = dict(zip(steps, rest[: len(steps)]))
    potential_ref = rest[len(steps)]
    out_groups = dict(zip(steps, rest[len(steps) + 1 :]))
    slots = tile_slots(pick_ref, me_ref[0], steps, devices, capacity)
    total = pair_density(slots, near_ref[...], full, table_ref, groups)
    valence = jnp.sum(total, axis=0, keepdims=True)
    value = jnp.maximum(core_ref[...] + valence, density_floor)
    root = jnp.exp(jnp.log(value) * (1.0 / 3.0))
    root = root - (root * root * root - value) / (3.0 * root * root)
    potential = -slater_factor * root
    potential_ref[...] = potential
    pair_partials(slots, weight_ref[...] * potential, table_ref, out_groups)


def near_partials_kernel(
    devices, capacity, steps, me_ref, pick_ref, table_ref, weight_ref, found_ref, *rest
):
    out_groups = dict(zip(steps, rest))
    potential_ref = rest[len(steps)]
    potential_ref[...] = found_ref[...]
    slots = tile_slots(pick_ref, me_ref[0], steps, devices, capacity)
    pair_partials(slots, weight_ref[...] * found_ref[...], table_ref, out_groups)


def sum_kernel(devices, capacity, dest_ref, me_ref, *rest):
    in_refs = rest[:devices]
    kohn_ref, pairs = rest[devices:]
    width = kohn_ref.shape[-1]
    for k in range(devices):
        pairs[k * capacity : (k + 1) * capacity] = in_refs[k][...]
    places = pair_places(dest_ref, me_ref[0], devices, capacity)
    for i in range(KB):
        kohn_ref[pl.ds(i * width, width), :] = pairs[places[2 * i]].astype(jnp.float32) + pairs[
            places[2 * i + 1]
        ].astype(jnp.float32)


def per_device(
    block_store,
    block_source,
    chem_pot,
    basis_values,
    core_density,
    point_weights,
    pair_dest,
    tile_pairs,
):
    stored = block_store[0]
    held_count, block_width, _ = stored.shape
    source = block_source[0, 0]
    atom_devices = lax.axis_size("atoms")
    devices = lax.axis_size("space")
    if pl.cdiv(source.shape[0], atom_devices) < held_count:
        blocks, place = requested_blocks(stored, source)
    else:
        blocks, place = gathered_blocks(stored, source)
    destinations = pair_dest[0, 0]
    send_count = destinations.shape[0]
    capacity = pl.cdiv(send_count, devices)
    order = KB * block_width
    me = lax.axis_index("space").reshape(1)
    group = jax.ShapeDtypeStruct((capacity, block_width, block_width), jnp.bfloat16)
    out = pl.pallas_call(
        functools.partial(sign_kernel, devices, capacity),
        name="sign",
        in_specs=[SMEM] * 4 + [VMEM],
        out_shape=[jax.ShapeDtypeStruct((order, block_width), jnp.bfloat16)] + [group] * devices,
        out_specs=[VMEM] * (1 + devices),
        scratch_shapes=[
            pltpu.VMEM((order, order), jnp.float32),
            pltpu.VMEM((order, order), jnp.bfloat16),
            pltpu.VMEM((order, order), jnp.bfloat16),
            pltpu.VMEM((order, order), jnp.bfloat16),
            pltpu.VMEM((devices * capacity, block_width, block_width), jnp.bfloat16),
        ],
        compiler_params=pltpu.CompilerParams(vmem_limit_bytes=16 << 20),
        cost_estimate=pl.CostEstimate(
            flops=4 * order**3, bytes_accessed=4 * order * order, transcendentals=0
        ),
    )(place, chem_pot, destinations, me, blocks)
    column = out[0]
    outgoing = dict(enumerate(out[1:]))
    near, far = range(min(2, devices)), range(min(2, devices), devices)
    incoming = exchange(outgoing, 1)
    tables = basis_values[0, 0]
    points = tables.shape[-1]
    full = devices * capacity == send_count
    pick = tile_pairs[0, 0]
    row = jax.ShapeDtypeStruct((1, points), jnp.float32)

    def cost(pairs):
        return pl.CostEstimate(
            flops=2 * pairs * block_width**2 * points,
            bytes_accessed=4 * pairs * block_width * points,
            transcendentals=0,
        )

    limit = pltpu.CompilerParams(vmem_limit_bytes=16 << 20)
    total, density = pl.pallas_call(
        functools.partial(near_density_kernel, devices, capacity, full, near),
        name="near_density",
        in_specs=[SMEM] * 2 + [VMEM] * (2 + len(near)),
        out_shape=[jax.ShapeDtypeStruct((8, points), jnp.float32), column],
        out_specs=[VMEM] * 2,
        compiler_params=limit,
        cost_estimate=cost(len(near) * capacity),
    )(me, pick, tables, column, *[incoming[k] for k in near])
    found, *sent = pl.pallas_call(
        functools.partial(far_kernel, devices, capacity, full, far),
        name="far",
        in_specs=[SMEM] * 2 + [VMEM] * (4 + len(far)),
        out_shape=[row] + [group] * len(far),
        out_specs=[VMEM] * (1 + len(far)),
        compiler_params=limit,
        cost_estimate=cost(2 * len(far) * capacity),
    )(
        me,
        pick,
        tables,
        core_density[0],
        point_weights[0],
        total,
        *[incoming[k] for k in far],
    )
    partials = dict(zip(far, sent))
    *sent, potential = pl.pallas_call(
        functools.partial(near_partials_kernel, devices, capacity, near),
        name="near_partials",
        in_specs=[SMEM] * 2 + [VMEM] * 3,
        out_shape=[group] * len(near) + [row],
        out_specs=[VMEM] * (len(near) + 1),
        compiler_params=limit,
        cost_estimate=cost(len(near) * capacity),
    )(me, pick, tables, point_weights[0], found)
    partials.update(zip(near, sent))
    returned = exchange(partials, -1)
    kohn = pl.pallas_call(
        functools.partial(sum_kernel, devices, capacity),
        name="sum",
        in_specs=[SMEM] * 2 + [VMEM] * devices,
        out_shape=jax.ShapeDtypeStruct((order, block_width), jnp.float32),
        out_specs=VMEM,
        scratch_shapes=[
            pltpu.VMEM((devices * capacity, block_width, block_width), jnp.bfloat16),
        ],
        compiler_params=pltpu.CompilerParams(vmem_limit_bytes=8 << 20),
    )(destinations, me, *[returned[k] for k in range(devices)])
    return (density[None, None], potential[None], kohn[None, None])


def solution(mesh):
    placed = (
        P("space", "atoms", None, None),
        P("atoms", "space", None),
        P(),
        P("atoms", "space", None, None, None),
        P("atoms", "space", None),
        P("atoms", "space", None),
        P("atoms", "space", None),
        P("atoms", "space", None, None),
    )

    return jax.shard_map(
        per_device,
        mesh=mesh,
        in_specs=placed,
        out_specs=(
            P("atoms", "space", None, None),
            P("atoms", "space", None),
            P("atoms", "space", None, None),
        ),
        check_vma=False,
    )
```

```python
import functools
import math

import jax
import jax.numpy as jnp
from jax import lax
from jax.experimental import pallas as pl
from jax.experimental.pallas import tpu as pltpu
from jax.sharding import PartitionSpec as P

KB = 6


slater_factor = math.pow(3.0 / math.pi, 1.0 / 3.0)
density_floor = 0.05

VMEM = pl.BlockSpec(memory_space=pltpu.VMEM)
SMEM = pl.BlockSpec(memory_space=pltpu.SMEM)


def earlier_count(labels):
    order = jnp.arange(labels.shape[0])
    earlier = (labels[None, :] == labels[:, None]) & (order[None, :] < order[:, None])
    return jnp.sum(earlier.astype(jnp.int32), axis=1)


def requested_blocks(stored, source):
    held_count, block_width, _ = stored.shape
    atom_devices = lax.axis_size("atoms")
    capacity = pl.cdiv(source.shape[0], atom_devices)
    peer_index = source // held_count
    local_index = source % held_count
    slot_index = peer_index * capacity + earlier_count(peer_index)
    wanted = jnp.full((atom_devices * capacity,), -1, jnp.int32).at[slot_index].set(local_index)
    requested = lax.all_to_all(
        wanted.reshape(atom_devices, capacity), "atoms", split_axis=0, concat_axis=0, tiled=True
    )
    flat_request = requested.reshape(-1)
    chosen = jnp.take(stored, jnp.clip(flat_request, 0, held_count - 1), axis=0)
    arrived = lax.all_to_all(
        chosen.reshape(atom_devices, capacity, block_width, block_width),
        "atoms",
        split_axis=0,
        concat_axis=0,
        tiled=True,
    )
    return arrived.reshape(atom_devices * capacity, block_width, block_width), slot_index


def gather_order(devices):
    return sorted(range(1, devices), key=lambda r: (r.bit_count(), -r))


def gathered_blocks(stored):
    devices = lax.axis_size("atoms")
    parts = [stored] + [None] * (devices - 1)
    for offset in gather_order(devices):
        step = 2 if offset == 3 else offset & -offset
        pairs = [(i, i ^ step) for i in range(devices)]
        parts[offset] = lax.ppermute(parts[offset ^ step], "atoms", pairs)
    return jnp.concatenate(parts, axis=0)


def partner(me, step, devices):
    if devices & (devices - 1) == 0:
        return me ^ abs(step)
    return (me + step) % devices


def step_to(me, other, devices):
    if devices & (devices - 1) == 0:
        return me ^ other
    return lax.rem(other - me + devices, devices)


def step_from(me, other, devices):
    if devices & (devices - 1) == 0:
        return me ^ other
    return lax.rem(me - other + devices, devices)


def exchange(groups, sign):
    devices = lax.axis_size("space")
    got = {}
    for step in sorted(groups, reverse=True):
        pairs = [(i, partner(i, sign * step, devices)) for i in range(devices)]
        got[step] = lax.ppermute(groups[step], "space", pairs) if step else groups[step]
    return got


def index_kernel(
    devices, capacity, held, slots, sends, table_ref, atom_ref, me_ref, chem_ref, row_ref, level_ref
):
    me = me_ref[0]
    table = table_ref[...]
    values = []
    for j in range(slots):
        place = table[0, j]
        if held:
            place = (atom_ref[0] ^ lax.div(place, held)) * held + lax.rem(place, held)
        values.append(place)
    dests = [table[0, slots + j] for j in range(sends)]
    for j, dest in enumerate(dests):
        rank = jnp.int32(0)
        for earlier in dests[:j]:
            rank += jnp.where(earlier == dest, 1, 0)
        values.append(step_to(me, dest, devices) * capacity + rank)
    for k in range(devices):
        owner = step_from(me, k, devices)
        for c in range(capacity):
            for side in range(2):
                at = slots + sends + side * devices * capacity
                value = table[0, at]
                for slot in range(1, devices * capacity):
                    value = jnp.where(owner * capacity + c == slot, table[0, at + slot], value)
                values.append(value)
    lanes = lax.broadcasted_iota(jnp.int32, row_ref.shape, 1)
    row = jnp.zeros(row_ref.shape, jnp.int32)
    for j, value in enumerate(values):
        row = jnp.where(lanes == j, value, row)
    row_ref[...] = row
    level_ref[...] = jnp.full(level_ref.shape, chem_ref[0], jnp.float32)


def pair_places(row, sends):
    return [row[0, KB * KB + j] for j in range(sends)]


def sign_kernel(
    devices, capacity, row_ref, level_ref, block_ref, density_ref, *rest
):
    out_refs = rest[:devices]
    shifted, x_zero, t_one, x_one, pairs = rest[devices:]
    width = block_ref.shape[-1]
    order = KB * width
    rows = lax.broadcasted_iota(jnp.int32, (width, width), 0)
    cols = lax.broadcasted_iota(jnp.int32, (width, width), 1)
    diagonal = rows == cols
    unit = jnp.where(diagonal, 1.0, 0.0)
    level = level_ref[...] * unit
    row = row_ref[...]

    def at(i):
        return pl.ds(i * width, width)

    total = jnp.zeros((8, width), jnp.float32)
    tiles = [(i, j) for i in range(KB) for j in range(i, KB)]
    for i, j in tiles:
        upper = block_ref[row[0, i * KB + j]].astype(jnp.float32)
        lower = block_ref[row[0, j * KB + i]].astype(jnp.float32)
        value = 0.5 * (upper + lower.T)
        if i == j:
            value = value - level
        shifted[at(i), at(j)] = value
        squares = (value * value).reshape(width // 8, 8, width).sum(axis=0)
        total = total + (squares if i == j else 2.0 * squares)
    mean = jnp.sum(total, keepdims=True) / order
    inverse = 1.0 / (2.0 * jnp.sqrt(mean + 1e-06))
    for i, j in tiles:
        value = (shifted[at(i), at(j)] * inverse).astype(jnp.bfloat16)
        x_zero[at(i), at(j)] = value
        if i != j:
            x_zero[at(j), at(i)] = value.T
    for i in range(KB):
        square = jnp.dot(x_zero[at(i), :], x_zero[...], preferred_element_type=jnp.float32)
        for j in range(KB):
            part = -0.5 * square[:, j * width : (j + 1) * width]
            t_one[at(i), at(j)] = (1.5 * unit + part if i == j else part).astype(jnp.bfloat16)
    for i in range(KB):
        x_one[at(i), :] = jnp.dot(
            x_zero[at(i), :], t_one[...], preferred_element_type=jnp.float32
        ).astype(jnp.bfloat16)
    square = jnp.dot(x_one[...], x_one[:, at(0)], preferred_element_type=jnp.float32)
    parts = []
    for i in range(KB):
        part = -0.5 * square[i * width : (i + 1) * width]
        parts.append((1.5 * unit + part if i == 0 else part).astype(jnp.bfloat16))
    t_two = jnp.concatenate(parts, axis=0)
    final = jnp.dot(x_one[...], t_two, preferred_element_type=jnp.float32)
    for i in range(KB):
        part = final[i * width : (i + 1) * width]
        density_ref[at(i), :] = (0.5 * (unit - part if i == 0 else -part)).astype(jnp.bfloat16)
    places = pair_places(row, 2 * KB)
    for j, place in enumerate(places):
        pairs[place] = density_ref[at(j // 2), :]
    for k in range(devices):
        out_refs[k][...] = pairs[k * capacity : (k + 1) * capacity]


def tile_slots(row, steps, capacity):
    slots = []
    for k in steps:
        for c in range(capacity):
            at = KB * KB + 2 * KB + 2 * (k * capacity + c)
            slots.append((k, c, row[0, at], row[0, at + 1]))
    return slots


def pair_density(slots, total, full, table_ref, group_refs):
    width, points = table_ref.shape[1:]
    for k, c, u, v in slots:
        left = table_ref[jnp.maximum(u, 0)].astype(jnp.float32)
        right = table_ref[jnp.maximum(v, 0)]
        product = jnp.dot(group_refs[k][c], right, preferred_element_type=jnp.float32)
        term = (left * product).reshape(width // 8, 8, points).sum(axis=0)
        total = total + term if full else jnp.where(u >= 0, total + term, total)
    return total


def pair_partials(slots, scaled, table_ref, group_refs):
    for k, c, u, v in slots:
        left = table_ref[jnp.maximum(u, 0)].astype(jnp.float32)
        right = table_ref[jnp.maximum(v, 0)]
        weighted = (left * scaled).astype(jnp.bfloat16)
        group_refs[k][c] = lax.dot_general(
            weighted, right, (((1,), (1,)), ((), ())), preferred_element_type=jnp.float32
        ).astype(jnp.bfloat16)


def near_density_kernel(
    capacity, full, steps, row_ref, table_ref, column_ref, *rest
):
    groups = dict(zip(steps, rest[: len(steps)]))
    total_ref, density_ref = rest[len(steps) :]
    density_ref[...] = column_ref[...]
    slots = tile_slots(row_ref[...], steps, capacity)
    total = jnp.zeros(total_ref.shape, jnp.float32)
    total_ref[...] = pair_density(slots, total, full, table_ref, groups)


def far_kernel(
    capacity, full, steps, row_ref, table_ref, core_ref, weight_ref, near_ref, *rest
):
    groups = dict(zip(steps, rest[: len(steps)]))
    potential_ref = rest[len(steps)]
    out_groups = dict(zip(steps, rest[len(steps) + 1 :]))
    slots = tile_slots(row_ref[...], steps, capacity)
    total = pair_density(slots, near_ref[...], full, table_ref, groups)
    valence = jnp.sum(total, axis=0, keepdims=True)
    value = jnp.maximum(core_ref[...] + valence, density_floor)
    root = jnp.exp(jnp.log(value) * (1.0 / 3.0))
    root = root - (root * root * root - value) / (3.0 * root * root)
    potential = -slater_factor * root
    potential_ref[...] = potential
    pair_partials(slots, weight_ref[...] * potential, table_ref, out_groups)


def near_partials_kernel(
    capacity, steps, row_ref, table_ref, weight_ref, found_ref, *rest
):
    out_groups = dict(zip(steps, rest))
    potential_ref = rest[len(steps)]
    potential_ref[...] = found_ref[...]
    slots = tile_slots(row_ref[...], steps, capacity)
    pair_partials(slots, weight_ref[...] * found_ref[...], table_ref, out_groups)


def sum_kernel(devices, capacity, row_ref, *rest):
    in_refs = rest[:devices]
    kohn_ref, pairs = rest[devices:]
    width = kohn_ref.shape[-1]
    for k in range(devices):
        pairs[k * capacity : (k + 1) * capacity] = in_refs[k][...]
    places = pair_places(row_ref[...], 2 * KB)
    for i in range(KB):
        kohn_ref[pl.ds(i * width, width), :] = pairs[places[2 * i]].astype(jnp.float32) + pairs[
            places[2 * i + 1]
        ].astype(jnp.float32)


def gathers(slot_count, devices, held_count):
    return devices & (devices - 1) == 0 and pl.cdiv(slot_count, devices) >= held_count


def per_device(
    block_store,
    block_source,
    chem_pot,
    basis_values,
    core_density,
    point_weights,
    pair_dest,
    tile_pairs,
):
    stored = block_store[0]
    held_count, block_width, _ = stored.shape
    source = block_source[0, 0]
    atom_devices = lax.axis_size("atoms")
    devices = lax.axis_size("space")
    destinations = pair_dest[0, 0]
    send_count = destinations.shape[0]
    capacity = pl.cdiv(send_count, devices)
    order = KB * block_width
    direct = gathers(source.shape[0], atom_devices, held_count)
    if direct:
        blocks = gathered_blocks(stored)
    else:
        blocks, source = requested_blocks(stored, source)
    length = source.shape[0] + send_count + 2 * devices * capacity
    length = pl.cdiv(length, 128) * 128
    table = jnp.concatenate([source, destinations, tile_pairs[0, 0].reshape(-1)])
    table = jnp.pad(table, (0, length - table.shape[0])).reshape(1, length)
    row, level = pl.pallas_call(
        functools.partial(
            index_kernel,
            devices,
            capacity,
            held_count if direct else 0,
            source.shape[0],
            send_count,
        ),
        name="index",
        in_specs=[VMEM] + [SMEM] * 3,
        out_shape=[
            jax.ShapeDtypeStruct((1, length), jnp.int32),
            jax.ShapeDtypeStruct((1, block_width), jnp.float32),
        ],
        out_specs=[VMEM] * 2,
        compiler_params=pltpu.CompilerParams(vmem_limit_bytes=1 << 20),
        cost_estimate=pl.CostEstimate(flops=2000, bytes_accessed=2000, transcendentals=0),
    )(
        table,
        lax.axis_index("atoms").reshape(1),
        lax.axis_index("space").reshape(1),
        chem_pot,
    )
    group = jax.ShapeDtypeStruct((capacity, block_width, block_width), jnp.bfloat16)
    out = pl.pallas_call(
        functools.partial(sign_kernel, devices, capacity),
        name="sign",
        in_specs=[VMEM] * 3,
        out_shape=[jax.ShapeDtypeStruct((order, block_width), jnp.bfloat16)] + [group] * devices,
        out_specs=[VMEM] * (1 + devices),
        scratch_shapes=[
            pltpu.VMEM((order, order), jnp.float32),
            pltpu.VMEM((order, order), jnp.bfloat16),
            pltpu.VMEM((order, order), jnp.bfloat16),
            pltpu.VMEM((order, order), jnp.bfloat16),
            pltpu.VMEM((devices * capacity, block_width, block_width), jnp.bfloat16),
        ],
        compiler_params=pltpu.CompilerParams(vmem_limit_bytes=16 << 20),
        cost_estimate=pl.CostEstimate(
            flops=4 * order**3, bytes_accessed=4 * order * order, transcendentals=0
        ),
    )(row, level, blocks)
    column = out[0]
    outgoing = dict(enumerate(out[1:]))
    near, far = range(min(2, devices)), range(min(2, devices), devices)
    incoming = exchange(outgoing, 1)
    tables = basis_values[0, 0]
    points = tables.shape[-1]
    full = devices * capacity == send_count
    line = jax.ShapeDtypeStruct((1, points), jnp.float32)

    def cost(pairs):
        return pl.CostEstimate(
            flops=2 * pairs * block_width**2 * points,
            bytes_accessed=4 * pairs * block_width * points,
            transcendentals=0,
        )

    limit = pltpu.CompilerParams(vmem_limit_bytes=16 << 20)
    total, density = pl.pallas_call(
        functools.partial(near_density_kernel, capacity, full, near),
        name="near_density",
        in_specs=[VMEM] * (3 + len(near)),
        out_shape=[jax.ShapeDtypeStruct((8, points), jnp.float32), column],
        out_specs=[VMEM] * 2,
        compiler_params=limit,
        cost_estimate=cost(len(near) * capacity),
    )(row, tables, column, *[incoming[k] for k in near])
    found, *sent = pl.pallas_call(
        functools.partial(far_kernel, capacity, full, far),
        name="far",
        in_specs=[VMEM] * (5 + len(far)),
        out_shape=[line] + [group] * len(far),
        out_specs=[VMEM] * (1 + len(far)),
        compiler_params=limit,
        cost_estimate=cost(2 * len(far) * capacity),
    )(
        row,
        tables,
        core_density[0],
        point_weights[0],
        total,
        *[incoming[k] for k in far],
    )
    partials = dict(zip(far, sent))
    *sent, potential = pl.pallas_call(
        functools.partial(near_partials_kernel, capacity, near),
        name="near_partials",
        in_specs=[VMEM] * 4,
        out_shape=[group] * len(near) + [line],
        out_specs=[VMEM] * (len(near) + 1),
        compiler_params=limit,
        cost_estimate=cost(len(near) * capacity),
    )(row, tables, point_weights[0], found)
    partials.update(zip(near, sent))
    returned = exchange(partials, -1)
    kohn = pl.pallas_call(
        functools.partial(sum_kernel, devices, capacity),
        name="sum",
        in_specs=[VMEM] * (1 + devices),
        out_shape=jax.ShapeDtypeStruct((order, block_width), jnp.float32),
        out_specs=VMEM,
        scratch_shapes=[
            pltpu.VMEM((devices * capacity, block_width, block_width), jnp.bfloat16),
        ],
        compiler_params=pltpu.CompilerParams(vmem_limit_bytes=8 << 20),
    )(row, *[returned[k] for k in range(devices)])
    return (density[None, None], potential[None], kohn[None, None])


def solution(mesh):
    placed = (
        P("space", "atoms", None, None),
        P("atoms", "space", None),
        P(),
        P("atoms", "space", None, None, None),
        P("atoms", "space", None),
        P("atoms", "space", None),
        P("atoms", "space", None),
        P("atoms", "space", None, None),
    )

    return jax.shard_map(
        per_device,
        mesh=mesh,
        in_specs=placed,
        out_specs=(
            P("atoms", "space", None, None),
            P("atoms", "space", None),
            P("atoms", "space", None, None),
        ),
        check_vma=False,
    )
```

```python
import functools
import math

import jax
import jax.numpy as jnp
from jax import lax
from jax.experimental import pallas as pl
from jax.experimental.pallas import tpu as pltpu
from jax.sharding import PartitionSpec as P

KB = 6


slater_factor = math.pow(3.0 / math.pi, 1.0 / 3.0)
density_floor = 0.05

VMEM = pl.BlockSpec(memory_space=pltpu.VMEM)
SMEM = pl.BlockSpec(memory_space=pltpu.SMEM)


def earlier_count(labels):
    order = jnp.arange(labels.shape[0])
    earlier = (labels[None, :] == labels[:, None]) & (order[None, :] < order[:, None])
    return jnp.sum(earlier.astype(jnp.int32), axis=1)


def requested_blocks(stored, source):
    held_count, block_width, _ = stored.shape
    atom_devices = lax.axis_size("atoms")
    capacity = pl.cdiv(source.shape[0], atom_devices)
    peer_index = source // held_count
    local_index = source % held_count
    slot_index = peer_index * capacity + earlier_count(peer_index)
    wanted = jnp.full((atom_devices * capacity,), -1, jnp.int32).at[slot_index].set(local_index)
    requested = lax.all_to_all(
        wanted.reshape(atom_devices, capacity), "atoms", split_axis=0, concat_axis=0, tiled=True
    )
    flat_request = requested.reshape(-1)
    chosen = jnp.take(stored, jnp.clip(flat_request, 0, held_count - 1), axis=0)
    arrived = lax.all_to_all(
        chosen.reshape(atom_devices, capacity, block_width, block_width),
        "atoms",
        split_axis=0,
        concat_axis=0,
        tiled=True,
    )
    return arrived.reshape(atom_devices * capacity, block_width, block_width), slot_index


def gather_order(devices):
    return sorted(range(1, devices), key=lambda r: (r.bit_count(), -r))


def gathered_blocks(stored):
    devices = lax.axis_size("atoms")
    parts = [stored] + [None] * (devices - 1)
    for offset in gather_order(devices):
        step = 2 if offset == 3 else offset & -offset
        pairs = [(i, i ^ step) for i in range(devices)]
        parts[offset] = lax.ppermute(parts[offset ^ step], "atoms", pairs)
    return jnp.concatenate(parts, axis=0)


def partner(me, step, devices):
    if devices & (devices - 1) == 0:
        return me ^ abs(step)
    return (me + step) % devices


def step_to(me, other, devices):
    if devices & (devices - 1) == 0:
        return me ^ other
    return lax.rem(other - me + devices, devices)


def step_from(me, other, devices):
    if devices & (devices - 1) == 0:
        return me ^ other
    return lax.rem(me - other + devices, devices)


def exchange(groups, sign):
    devices = lax.axis_size("space")
    got = {}
    for step in sorted(groups, reverse=True):
        pairs = [(i, partner(i, sign * step, devices)) for i in range(devices)]
        got[step] = lax.ppermute(groups[step], "space", pairs) if step else groups[step]
    return got


def index_kernel(
    devices, capacity, held, slots, sends, table_ref, atom_ref, me_ref, chem_ref, row_ref, level_ref
):
    me = me_ref[0]
    table = table_ref[...]
    values = []
    for j in range(slots):
        place = table[0, j]
        if held:
            place = (atom_ref[0] ^ lax.div(place, held)) * held + lax.rem(place, held)
        values.append(place)
    dests = [table[0, slots + j] for j in range(sends)]
    for j, dest in enumerate(dests):
        rank = jnp.int32(0)
        for earlier in dests[:j]:
            rank += jnp.where(earlier == dest, 1, 0)
        values.append(step_to(me, dest, devices) * capacity + rank)
    for k in range(devices):
        owner = step_from(me, k, devices)
        for c in range(capacity):
            for side in range(2):
                at = slots + sends + side * devices * capacity
                value = table[0, at]
                for slot in range(1, devices * capacity):
                    value = jnp.where(owner * capacity + c == slot, table[0, at + slot], value)
                values.append(value)
    lanes = lax.broadcasted_iota(jnp.int32, row_ref.shape, 1)
    row = jnp.zeros(row_ref.shape, jnp.int32)
    for j, value in enumerate(values):
        row = jnp.where(lanes == j, value, row)
    row_ref[...] = row
    level_ref[...] = jnp.full(level_ref.shape, chem_ref[0], jnp.float32)


def pair_places(row, sends):
    return [row[0, KB * KB + j] for j in range(sends)]


def sign_kernel(
    devices, capacity, row_ref, level_ref, block_ref, density_ref, *rest
):
    out_refs = rest[:devices]
    shifted, x_zero, t_one, x_one, pairs = rest[devices:]
    width = block_ref.shape[-1]
    order = KB * width
    rows = lax.broadcasted_iota(jnp.int32, (width, width), 0)
    cols = lax.broadcasted_iota(jnp.int32, (width, width), 1)
    diagonal = rows == cols
    unit = jnp.where(diagonal, 1.0, 0.0)
    level = level_ref[...] * unit
    row = row_ref[...]

    def at(i):
        return pl.ds(i * width, width)

    total = jnp.zeros((8, width), jnp.float32)
    tiles = [(i, j) for i in range(KB) for j in range(i, KB)]
    for i, j in tiles:
        upper = block_ref[row[0, i * KB + j]].astype(jnp.float32)
        lower = block_ref[row[0, j * KB + i]].astype(jnp.float32)
        value = 0.5 * (upper + lower.T)
        if i == j:
            value = value - level
        shifted[at(i), at(j)] = value
        squares = (value * value).reshape(width // 8, 8, width).sum(axis=0)
        total = total + (squares if i == j else 2.0 * squares)
    mean = jnp.sum(total, keepdims=True) / order
    inverse = 1.0 / (2.0 * jnp.sqrt(mean + 1e-06))
    for i, j in tiles:
        value = (shifted[at(i), at(j)] * inverse).astype(jnp.bfloat16)
        x_zero[at(i), at(j)] = value
        if i != j:
            x_zero[at(j), at(i)] = value.T
    for i in range(0, KB, 2):
        pair = pl.ds(i * width, 2 * width)
        right = pl.ds(i * width, order - i * width)
        square = jnp.dot(x_zero[pair, :], x_zero[:, right], preferred_element_type=jnp.float32)
        for k in (i, i + 1):
            for j in range(i, KB):
                rows, cols = (k - i) * width, (j - i) * width
                part = -0.5 * square[rows : rows + width, cols : cols + width]
                value = (1.5 * unit + part if k == j else part).astype(jnp.bfloat16)
                t_one[at(k), at(j)] = value
                if j > i + 1:
                    t_one[at(j), at(k)] = value.T
    for i in range(0, KB, 2):
        pair = pl.ds(i * width, 2 * width)
        right = pl.ds(i * width, order - i * width)
        value = jnp.dot(
            x_zero[pair, :], t_one[:, right], preferred_element_type=jnp.float32
        ).astype(jnp.bfloat16)
        x_one[pair, right] = value
        if i + 2 < KB:
            below = pl.ds((i + 2) * width, order - (i + 2) * width)
            x_one[below, pair] = value[:, 2 * width :].T
    square = jnp.dot(x_one[...], x_one[:, at(0)], preferred_element_type=jnp.float32)
    parts = []
    for i in range(KB):
        part = -0.5 * square[i * width : (i + 1) * width]
        parts.append((1.5 * unit + part if i == 0 else part).astype(jnp.bfloat16))
    t_two = jnp.concatenate(parts, axis=0)
    final = jnp.dot(x_one[...], t_two, preferred_element_type=jnp.float32)
    for i in range(KB):
        part = final[i * width : (i + 1) * width]
        density_ref[at(i), :] = (0.5 * (unit - part if i == 0 else -part)).astype(jnp.bfloat16)
    places = pair_places(row, 2 * KB)
    for j, place in enumerate(places):
        pairs[place] = density_ref[at(j // 2), :]
    for k in range(devices):
        out_refs[k][...] = pairs[k * capacity : (k + 1) * capacity]


def tile_slots(row, steps, capacity):
    slots = []
    for k in steps:
        for c in range(capacity):
            at = KB * KB + 2 * KB + 2 * (k * capacity + c)
            slots.append((k, c, row[0, at], row[0, at + 1]))
    return slots


def pair_density(slots, total, full, table_ref, group_refs):
    width, points = table_ref.shape[1:]
    for k, c, u, v in slots:
        left = table_ref[jnp.maximum(u, 0)].astype(jnp.float32)
        right = table_ref[jnp.maximum(v, 0)]
        product = jnp.dot(group_refs[k][c], right, preferred_element_type=jnp.float32)
        term = (left * product).reshape(width // 8, 8, points).sum(axis=0)
        total = total + term if full else jnp.where(u >= 0, total + term, total)
    return total


def pair_partials(slots, scaled, table_ref, group_refs):
    for k, c, u, v in slots:
        left = table_ref[jnp.maximum(u, 0)].astype(jnp.float32)
        right = table_ref[jnp.maximum(v, 0)]
        weighted = (left * scaled).astype(jnp.bfloat16)
        group_refs[k][c] = lax.dot_general(
            weighted, right, (((1,), (1,)), ((), ())), preferred_element_type=jnp.float32
        ).astype(jnp.bfloat16)


def near_density_kernel(
    capacity, full, steps, row_ref, table_ref, column_ref, *rest
):
    groups = dict(zip(steps, rest[: len(steps)]))
    total_ref, density_ref = rest[len(steps) :]
    density_ref[...] = column_ref[...]
    slots = tile_slots(row_ref[...], steps, capacity)
    total = jnp.zeros(total_ref.shape, jnp.float32)
    total_ref[...] = pair_density(slots, total, full, table_ref, groups)


def mid_density_kernel(capacity, full, steps, row_ref, table_ref, near_ref, *rest):
    groups = dict(zip(steps, rest))
    slots = tile_slots(row_ref[...], steps, capacity)
    rest[-1][...] = pair_density(slots, near_ref[...], full, table_ref, groups)


def mid_partials_kernel(capacity, steps, row_ref, table_ref, weight_ref, found_ref, *rest):
    slots = tile_slots(row_ref[...], steps, capacity)
    pair_partials(slots, weight_ref[...] * found_ref[...], table_ref, dict(zip(steps, rest)))


def last_kernel(
    capacity, full, steps, row_ref, table_ref, core_ref, weight_ref, near_ref, *rest
):
    groups = dict(zip(steps, rest[: len(steps)]))
    potential_ref = rest[len(steps)]
    out_groups = dict(zip(steps, rest[len(steps) + 1 :]))
    slots = tile_slots(row_ref[...], steps, capacity)
    total = pair_density(slots, near_ref[...], full, table_ref, groups)
    valence = jnp.sum(total, axis=0, keepdims=True)
    value = jnp.maximum(core_ref[...] + valence, density_floor)
    root = jnp.exp(jnp.log(value) * (1.0 / 3.0))
    root = root - (root * root * root - value) / (3.0 * root * root)
    potential = -slater_factor * root
    potential_ref[...] = potential
    pair_partials(slots, weight_ref[...] * potential, table_ref, out_groups)


def near_partials_kernel(
    capacity, steps, row_ref, table_ref, weight_ref, found_ref, *rest
):
    out_groups = dict(zip(steps, rest))
    potential_ref = rest[len(steps)]
    potential_ref[...] = found_ref[...]
    slots = tile_slots(row_ref[...], steps, capacity)
    pair_partials(slots, weight_ref[...] * found_ref[...], table_ref, out_groups)


def sum_kernel(devices, capacity, row_ref, *rest):
    in_refs = rest[:devices]
    kohn_ref, pairs = rest[devices:]
    width = kohn_ref.shape[-1]
    for k in range(devices):
        pairs[k * capacity : (k + 1) * capacity] = in_refs[k][...]
    places = pair_places(row_ref[...], 2 * KB)
    for i in range(KB):
        kohn_ref[pl.ds(i * width, width), :] = pairs[places[2 * i]].astype(jnp.float32) + pairs[
            places[2 * i + 1]
        ].astype(jnp.float32)


def gathers(slot_count, devices, held_count):
    return devices & (devices - 1) == 0 and pl.cdiv(slot_count, devices) >= held_count


def per_device(
    block_store,
    block_source,
    chem_pot,
    basis_values,
    core_density,
    point_weights,
    pair_dest,
    tile_pairs,
):
    stored = block_store[0]
    held_count, block_width, _ = stored.shape
    source = block_source[0, 0]
    atom_devices = lax.axis_size("atoms")
    devices = lax.axis_size("space")
    destinations = pair_dest[0, 0]
    send_count = destinations.shape[0]
    capacity = pl.cdiv(send_count, devices)
    order = KB * block_width
    direct = gathers(source.shape[0], atom_devices, held_count)
    if direct:
        blocks = gathered_blocks(stored)
    else:
        blocks, source = requested_blocks(stored, source)
    length = source.shape[0] + send_count + 2 * devices * capacity
    length = pl.cdiv(length, 128) * 128
    table = jnp.concatenate([source, destinations, tile_pairs[0, 0].reshape(-1)])
    table = jnp.pad(table, (0, length - table.shape[0])).reshape(1, length)
    row, level = pl.pallas_call(
        functools.partial(
            index_kernel,
            devices,
            capacity,
            held_count if direct else 0,
            source.shape[0],
            send_count,
        ),
        name="index",
        in_specs=[VMEM] + [SMEM] * 3,
        out_shape=[
            jax.ShapeDtypeStruct((1, length), jnp.int32),
            jax.ShapeDtypeStruct((1, block_width), jnp.float32),
        ],
        out_specs=[VMEM] * 2,
        compiler_params=pltpu.CompilerParams(vmem_limit_bytes=1 << 20),
        cost_estimate=pl.CostEstimate(flops=2000, bytes_accessed=2000, transcendentals=0),
    )(
        table,
        lax.axis_index("atoms").reshape(1),
        lax.axis_index("space").reshape(1),
        chem_pot,
    )
    group = jax.ShapeDtypeStruct((capacity, block_width, block_width), jnp.bfloat16)
    out = pl.pallas_call(
        functools.partial(sign_kernel, devices, capacity),
        name="sign",
        in_specs=[VMEM] * 3,
        out_shape=[jax.ShapeDtypeStruct((order, block_width), jnp.bfloat16)] + [group] * devices,
        out_specs=[VMEM] * (1 + devices),
        scratch_shapes=[
            pltpu.VMEM((order, order), jnp.float32),
            pltpu.VMEM((order, order), jnp.bfloat16),
            pltpu.VMEM((order, order), jnp.bfloat16),
            pltpu.VMEM((order, order), jnp.bfloat16),
            pltpu.VMEM((devices * capacity, block_width, block_width), jnp.bfloat16),
        ],
        compiler_params=pltpu.CompilerParams(vmem_limit_bytes=16 << 20),
        cost_estimate=pl.CostEstimate(
            flops=4 * order**3, bytes_accessed=4 * order * order, transcendentals=0
        ),
    )(row, level, blocks)
    column = out[0]
    outgoing = dict(enumerate(out[1:]))
    near, mid, last = range(2), range(2, devices - 1), range(devices - 1, devices)
    incoming = exchange(outgoing, 1)
    tables = basis_values[0, 0]
    points = tables.shape[-1]
    full = devices * capacity == send_count
    line = jax.ShapeDtypeStruct((1, points), jnp.float32)
    lines = jax.ShapeDtypeStruct((8, points), jnp.float32)

    def step_call(kernel, steps, out_shape, operands):
        pairs = len(steps) * capacity
        return pl.pallas_call(
            kernel,
            in_specs=[VMEM] * len(operands),
            out_shape=out_shape,
            out_specs=[VMEM] * len(out_shape),
            compiler_params=pltpu.CompilerParams(vmem_limit_bytes=16 << 20),
            cost_estimate=pl.CostEstimate(
                flops=2 * pairs * block_width**2 * points,
                bytes_accessed=4 * pairs * block_width * points,
                transcendentals=0,
            ),
        )(*operands)

    total, density = step_call(
        functools.partial(near_density_kernel, capacity, full, near),
        near,
        [lines, column],
        [row, tables, column, *[incoming[k] for k in near]],
    )
    (total,) = step_call(
        functools.partial(mid_density_kernel, capacity, full, mid),
        mid,
        [lines],
        [row, tables, total, *[incoming[k] for k in mid]],
    )
    weight = point_weights[0]
    found, *sent = step_call(
        functools.partial(last_kernel, capacity, full, last),
        last,
        [line] + [group] * len(last),
        [row, tables, core_density[0], weight, total, *[incoming[k] for k in last]],
    )
    partials = dict(zip(last, sent))
    sent = step_call(
        functools.partial(mid_partials_kernel, capacity, mid),
        mid,
        [group] * len(mid),
        [row, tables, weight, found],
    )
    partials.update(zip(mid, sent))
    *sent, potential = step_call(
        functools.partial(near_partials_kernel, capacity, near),
        near,
        [group] * len(near) + [line],
        [row, tables, weight, found],
    )
    partials.update(zip(near, sent))
    returned = exchange(partials, -1)
    kohn = pl.pallas_call(
        functools.partial(sum_kernel, devices, capacity),
        name="sum",
        in_specs=[VMEM] * (1 + devices),
        out_shape=jax.ShapeDtypeStruct((order, block_width), jnp.float32),
        out_specs=VMEM,
        scratch_shapes=[
            pltpu.VMEM((devices * capacity, block_width, block_width), jnp.bfloat16),
        ],
        compiler_params=pltpu.CompilerParams(vmem_limit_bytes=8 << 20),
    )(row, *[returned[k] for k in range(devices)])
    return (density[None, None], potential[None], kohn[None, None])


def solution(mesh):
    placed = (
        P("space", "atoms", None, None),
        P("atoms", "space", None),
        P(),
        P("atoms", "space", None, None, None),
        P("atoms", "space", None),
        P("atoms", "space", None),
        P("atoms", "space", None),
        P("atoms", "space", None, None),
    )

    return jax.shard_map(
        per_device,
        mesh=mesh,
        in_specs=placed,
        out_specs=(
            P("atoms", "space", None, None),
            P("atoms", "space", None),
            P("atoms", "space", None, None),
        ),
        check_vma=False,
    )
```

```python
import functools
import math

import jax
import jax.numpy as jnp
from jax import lax
from jax.experimental import pallas as pl
from jax.experimental.pallas import tpu as pltpu
from jax.sharding import PartitionSpec as P

KB = 6


slater_factor = math.pow(3.0 / math.pi, 1.0 / 3.0)
density_floor = 0.05

VMEM = pl.BlockSpec(memory_space=pltpu.VMEM)
SMEM = pl.BlockSpec(memory_space=pltpu.SMEM)


def earlier_count(labels):
    order = jnp.arange(labels.shape[0])
    earlier = (labels[None, :] == labels[:, None]) & (order[None, :] < order[:, None])
    return jnp.sum(earlier.astype(jnp.int32), axis=1)


def requested_blocks(stored, source):
    held_count, block_width, _ = stored.shape
    atom_devices = lax.axis_size("atoms")
    capacity = pl.cdiv(source.shape[0], atom_devices)
    peer_index = source // held_count
    local_index = source % held_count
    slot_index = peer_index * capacity + earlier_count(peer_index)
    wanted = jnp.full((atom_devices * capacity,), -1, jnp.int32).at[slot_index].set(local_index)
    requested = lax.all_to_all(
        wanted.reshape(atom_devices, capacity), "atoms", split_axis=0, concat_axis=0, tiled=True
    )
    flat_request = requested.reshape(-1)
    chosen = jnp.take(stored, jnp.clip(flat_request, 0, held_count - 1), axis=0)
    arrived = lax.all_to_all(
        chosen.reshape(atom_devices, capacity, block_width, block_width),
        "atoms",
        split_axis=0,
        concat_axis=0,
        tiled=True,
    )
    return arrived.reshape(atom_devices * capacity, block_width, block_width), slot_index


def gather_order(devices):
    return sorted(range(1, devices), key=lambda r: (r.bit_count(), -r))


def gathered_blocks(stored):
    devices = lax.axis_size("atoms")
    parts = [stored] + [None] * (devices - 1)
    for offset in gather_order(devices):
        step = 2 if offset == 3 else offset & -offset
        pairs = [(i, i ^ step) for i in range(devices)]
        parts[offset] = lax.ppermute(parts[offset ^ step], "atoms", pairs)
    return jnp.concatenate(parts, axis=0)


def partner(me, step, devices):
    if devices & (devices - 1) == 0:
        return me ^ abs(step)
    return (me + step) % devices


def step_to(me, other, devices):
    if devices & (devices - 1) == 0:
        return me ^ other
    return lax.rem(other - me + devices, devices)


def step_from(me, other, devices):
    if devices & (devices - 1) == 0:
        return me ^ other
    return lax.rem(me - other + devices, devices)


def exchange(groups, sign):
    devices = lax.axis_size("space")
    got = {}
    for step in sorted(groups, reverse=True):
        pairs = [(i, partner(i, sign * step, devices)) for i in range(devices)]
        got[step] = lax.ppermute(groups[step], "space", pairs) if step else groups[step]
    return got


def index_kernel(
    devices, capacity, held, slots, sends, table_ref, atom_ref, me_ref, chem_ref, row_ref, level_ref
):
    me = me_ref[0]
    table = table_ref[...]
    values = []
    for j in range(slots):
        place = table[0, j]
        if held:
            place = (atom_ref[0] ^ lax.div(place, held)) * held + lax.rem(place, held)
        values.append(place)
    dests = [table[0, slots + j] for j in range(sends)]
    for j, dest in enumerate(dests):
        rank = jnp.int32(0)
        for earlier in dests[:j]:
            rank += jnp.where(earlier == dest, 1, 0)
        values.append(step_to(me, dest, devices) * capacity + rank)
    for k in range(devices):
        owner = step_from(me, k, devices)
        for c in range(capacity):
            for side in range(2):
                at = slots + sends + side * devices * capacity
                value = table[0, at]
                for slot in range(1, devices * capacity):
                    value = jnp.where(owner * capacity + c == slot, table[0, at + slot], value)
                values.append(value)
    lanes = lax.broadcasted_iota(jnp.int32, row_ref.shape, 1)
    row = jnp.zeros(row_ref.shape, jnp.int32)
    for j, value in enumerate(values):
        row = jnp.where(lanes == j, value, row)
    row_ref[...] = row
    level_ref[...] = jnp.full(level_ref.shape, chem_ref[0], jnp.float32)


def pair_places(row, sends):
    return [row[0, KB * KB + j] for j in range(sends)]


def sign_kernel(
    devices, capacity, row_ref, level_ref, block_ref, density_ref, *rest
):
    out_refs = rest[:devices]
    shifted, x_zero, t_one, x_one, pairs = rest[devices:]
    width = block_ref.shape[-1]
    order = KB * width
    rows = lax.broadcasted_iota(jnp.int32, (width, width), 0)
    cols = lax.broadcasted_iota(jnp.int32, (width, width), 1)
    diagonal = rows == cols
    unit = jnp.where(diagonal, 1.0, 0.0)
    level = level_ref[...] * unit
    row = row_ref[...]

    def at(i):
        return pl.ds(i * width, width)

    total = jnp.zeros((8, width), jnp.float32)
    tiles = [(i, j) for i in range(KB) for j in range(i, KB)]
    for i, j in tiles:
        upper = block_ref[row[0, i * KB + j]].astype(jnp.float32)
        lower = block_ref[row[0, j * KB + i]].astype(jnp.float32)
        value = 0.5 * (upper + lower.T)
        if i == j:
            value = value - level
        shifted[at(i), at(j)] = value
        squares = (value * value).reshape(width // 8, 8, width).sum(axis=0)
        total = total + (squares if i == j else 2.0 * squares)
    mean = jnp.sum(total, keepdims=True) / order
    inverse = 1.0 / (2.0 * jnp.sqrt(mean + 1e-06))
    for i, j in tiles:
        value = (shifted[at(i), at(j)] * inverse).astype(jnp.bfloat16)
        x_zero[at(i), at(j)] = value
        if i != j:
            x_zero[at(j), at(i)] = value.T
    for i in range(0, KB, 2):
        pair = pl.ds(i * width, 2 * width)
        right = pl.ds(i * width, order - i * width)
        square = jnp.dot(x_zero[pair, :], x_zero[:, right], preferred_element_type=jnp.float32)
        for k in (i, i + 1):
            for j in range(i, KB):
                rows, cols = (k - i) * width, (j - i) * width
                part = -0.5 * square[rows : rows + width, cols : cols + width]
                value = (1.5 * unit + part if k == j else part).astype(jnp.bfloat16)
                t_one[at(k), at(j)] = value
                if j > i + 1:
                    t_one[at(j), at(k)] = value.T
    for i in range(0, KB, 2):
        pair = pl.ds(i * width, 2 * width)
        right = pl.ds(i * width, order - i * width)
        value = jnp.dot(
            x_zero[pair, :], t_one[:, right], preferred_element_type=jnp.float32
        ).astype(jnp.bfloat16)
        x_one[pair, right] = value
        if i + 2 < KB:
            below = pl.ds((i + 2) * width, order - (i + 2) * width)
            x_one[below, pair] = value[:, 2 * width :].T
    square = jnp.dot(x_one[...], x_one[:, at(0)], preferred_element_type=jnp.float32)
    parts = []
    for i in range(KB):
        part = -0.5 * square[i * width : (i + 1) * width]
        parts.append((1.5 * unit + part if i == 0 else part).astype(jnp.bfloat16))
    t_two = jnp.concatenate(parts, axis=0)
    final = jnp.dot(x_one[...], t_two, preferred_element_type=jnp.float32)
    for i in range(KB):
        part = final[i * width : (i + 1) * width]
        density_ref[at(i), :] = (0.5 * (unit - part if i == 0 else -part)).astype(jnp.bfloat16)
    places = pair_places(row, 2 * KB)
    for j, place in enumerate(places):
        pairs[place] = density_ref[at(j // 2), :]
    for k in range(devices):
        out_refs[k][...] = pairs[k * capacity : (k + 1) * capacity]


def tile_slots(row, steps, capacity):
    slots = []
    for k in steps:
        for c in range(capacity):
            at = KB * KB + 2 * KB + 2 * (k * capacity + c)
            slots.append((k, c, row[0, at], row[0, at + 1]))
    return slots


def pair_density(slots, total, full, table_ref, group_refs):
    width, points = table_ref.shape[1:]
    for k, c, u, v in slots:
        left = table_ref[jnp.maximum(u, 0)].astype(jnp.float32)
        right = table_ref[jnp.maximum(v, 0)]
        product = jnp.dot(group_refs[k][c], right, preferred_element_type=jnp.float32)
        term = (left * product).reshape(width // 8, 8, points).sum(axis=0)
        total = total + term if full else jnp.where(u >= 0, total + term, total)
    return total


def pair_partials(slots, scaled, table_ref, group_refs):
    for k, c, u, v in slots:
        left = table_ref[jnp.maximum(u, 0)].astype(jnp.float32)
        right = table_ref[jnp.maximum(v, 0)]
        weighted = (left * scaled).astype(jnp.bfloat16)
        group_refs[k][c] = lax.dot_general(
            weighted, right, (((1,), (1,)), ((), ())), preferred_element_type=jnp.float32
        ).astype(jnp.bfloat16)


def near_density_kernel(
    capacity, full, steps, row_ref, table_ref, column_ref, *rest
):
    groups = dict(zip(steps, rest[: len(steps)]))
    total_ref, density_ref = rest[len(steps) :]
    density_ref[...] = column_ref[...]
    slots = tile_slots(row_ref[...], steps, capacity)
    total = jnp.zeros(total_ref.shape, jnp.float32)
    total_ref[...] = pair_density(slots, total, full, table_ref, groups)


def mid_density_kernel(capacity, full, steps, row_ref, table_ref, near_ref, *rest):
    groups = dict(zip(steps, rest))
    slots = tile_slots(row_ref[...], steps, capacity)
    rest[-1][...] = pair_density(slots, near_ref[...], full, table_ref, groups)


def partials_kernel(capacity, steps, row_ref, table_ref, weight_ref, found_ref, *rest):
    slots = tile_slots(row_ref[...], steps, capacity)
    pair_partials(slots, weight_ref[...] * found_ref[...], table_ref, dict(zip(steps, rest)))


def last_kernel(
    capacity, full, steps, out_steps, row_ref, table_ref, core_ref, weight_ref, near_ref, *rest
):
    groups = dict(zip(steps, rest[: len(steps)]))
    potential_ref = rest[len(steps)]
    out_groups = dict(zip(out_steps, rest[len(steps) + 1 :]))
    slots = tile_slots(row_ref[...], steps, capacity)
    out_slots = tile_slots(row_ref[...], out_steps, capacity)
    total = pair_density(slots, near_ref[...], full, table_ref, groups)
    valence = jnp.sum(total, axis=0, keepdims=True)
    value = jnp.maximum(core_ref[...] + valence, density_floor)
    root = jnp.exp(jnp.log(value) * (1.0 / 3.0))
    root = root - (root * root * root - value) / (3.0 * root * root)
    potential = -slater_factor * root
    potential_ref[...] = potential
    pair_partials(out_slots, weight_ref[...] * potential, table_ref, out_groups)


def near_partials_kernel(
    capacity, steps, row_ref, table_ref, weight_ref, found_ref, *rest
):
    out_groups = dict(zip(steps, rest))
    potential_ref = rest[len(steps)]
    potential_ref[...] = found_ref[...]
    slots = tile_slots(row_ref[...], steps, capacity)
    pair_partials(slots, weight_ref[...] * found_ref[...], table_ref, out_groups)


def sum_kernel(devices, capacity, row_ref, *rest):
    in_refs = rest[:devices]
    kohn_ref, pairs = rest[devices:]
    width = kohn_ref.shape[-1]
    for k in range(devices):
        pairs[k * capacity : (k + 1) * capacity] = in_refs[k][...]
    places = pair_places(row_ref[...], 2 * KB)
    for i in range(KB):
        kohn_ref[pl.ds(i * width, width), :] = pairs[places[2 * i]].astype(jnp.float32) + pairs[
            places[2 * i + 1]
        ].astype(jnp.float32)


def gathers(slot_count, devices, held_count):
    return devices & (devices - 1) == 0 and pl.cdiv(slot_count, devices) >= held_count


def per_device(
    block_store,
    block_source,
    chem_pot,
    basis_values,
    core_density,
    point_weights,
    pair_dest,
    tile_pairs,
):
    stored = block_store[0]
    held_count, block_width, _ = stored.shape
    source = block_source[0, 0]
    atom_devices = lax.axis_size("atoms")
    devices = lax.axis_size("space")
    destinations = pair_dest[0, 0]
    send_count = destinations.shape[0]
    capacity = pl.cdiv(send_count, devices)
    order = KB * block_width
    direct = gathers(source.shape[0], atom_devices, held_count)
    if direct:
        blocks = gathered_blocks(stored)
    else:
        blocks, source = requested_blocks(stored, source)
    length = source.shape[0] + send_count + 2 * devices * capacity
    length = pl.cdiv(length, 128) * 128
    table = jnp.concatenate([source, destinations, tile_pairs[0, 0].reshape(-1)])
    table = jnp.pad(table, (0, length - table.shape[0])).reshape(1, length)
    row, level = pl.pallas_call(
        functools.partial(
            index_kernel,
            devices,
            capacity,
            held_count if direct else 0,
            source.shape[0],
            send_count,
        ),
        name="index",
        in_specs=[VMEM] + [SMEM] * 3,
        out_shape=[
            jax.ShapeDtypeStruct((1, length), jnp.int32),
            jax.ShapeDtypeStruct((1, block_width), jnp.float32),
        ],
        out_specs=[VMEM] * 2,
        compiler_params=pltpu.CompilerParams(vmem_limit_bytes=1 << 20),
        cost_estimate=pl.CostEstimate(flops=2000, bytes_accessed=2000, transcendentals=0),
    )(
        table,
        lax.axis_index("atoms").reshape(1),
        lax.axis_index("space").reshape(1),
        chem_pot,
    )
    group = jax.ShapeDtypeStruct((capacity, block_width, block_width), jnp.bfloat16)
    out = pl.pallas_call(
        functools.partial(sign_kernel, devices, capacity),
        name="sign",
        in_specs=[VMEM] * 3,
        out_shape=[jax.ShapeDtypeStruct((order, block_width), jnp.bfloat16)] + [group] * devices,
        out_specs=[VMEM] * (1 + devices),
        scratch_shapes=[
            pltpu.VMEM((order, order), jnp.float32),
            pltpu.VMEM((order, order), jnp.bfloat16),
            pltpu.VMEM((order, order), jnp.bfloat16),
            pltpu.VMEM((order, order), jnp.bfloat16),
            pltpu.VMEM((devices * capacity, block_width, block_width), jnp.bfloat16),
        ],
        compiler_params=pltpu.CompilerParams(vmem_limit_bytes=16 << 20),
        cost_estimate=pl.CostEstimate(
            flops=4 * order**3, bytes_accessed=4 * order * order, transcendentals=0
        ),
    )(row, level, blocks)
    column = out[0]
    outgoing = dict(enumerate(out[1:]))
    near, mid, last = range(2), range(2, devices - 1), range(devices - 1, devices)
    incoming = exchange(outgoing, 1)
    tables = basis_values[0, 0]
    points = tables.shape[-1]
    full = devices * capacity == send_count
    line = jax.ShapeDtypeStruct((1, points), jnp.float32)
    lines = jax.ShapeDtypeStruct((8, points), jnp.float32)

    def step_call(kernel, steps, out_shape, operands):
        pairs = len(steps) * capacity
        return pl.pallas_call(
            kernel,
            in_specs=[VMEM] * len(operands),
            out_shape=out_shape,
            out_specs=[VMEM] * len(out_shape),
            compiler_params=pltpu.CompilerParams(vmem_limit_bytes=16 << 20),
            cost_estimate=pl.CostEstimate(
                flops=2 * pairs * block_width**2 * points,
                bytes_accessed=4 * pairs * block_width * points,
                transcendentals=0,
            ),
        )(*operands)

    total, density = step_call(
        functools.partial(near_density_kernel, capacity, full, near),
        near,
        [lines, column],
        [row, tables, column, *[incoming[k] for k in near]],
    )
    (total,) = step_call(
        functools.partial(mid_density_kernel, capacity, full, mid),
        mid,
        [lines],
        [row, tables, total, *[incoming[k] for k in mid]],
    )
    weight = point_weights[0]
    found, *sent = step_call(
        functools.partial(last_kernel, capacity, full, last, mid),
        last,
        [line] + [group] * len(mid),
        [row, tables, core_density[0], weight, total, *[incoming[k] for k in last]],
    )
    partials = dict(zip(mid, sent))
    sent = step_call(
        functools.partial(partials_kernel, capacity, last),
        last,
        [group] * len(last),
        [row, tables, weight, found],
    )
    partials.update(zip(last, sent))
    *sent, potential = step_call(
        functools.partial(near_partials_kernel, capacity, near),
        near,
        [group] * len(near) + [line],
        [row, tables, weight, found],
    )
    partials.update(zip(near, sent))
    returned = exchange(partials, -1)
    kohn = pl.pallas_call(
        functools.partial(sum_kernel, devices, capacity),
        name="sum",
        in_specs=[VMEM] * (1 + devices),
        out_shape=jax.ShapeDtypeStruct((order, block_width), jnp.float32),
        out_specs=VMEM,
        scratch_shapes=[
            pltpu.VMEM((devices * capacity, block_width, block_width), jnp.bfloat16),
        ],
        compiler_params=pltpu.CompilerParams(vmem_limit_bytes=8 << 20),
    )(row, *[returned[k] for k in range(devices)])
    return (density[None, None], potential[None], kohn[None, None])


def solution(mesh):
    placed = (
        P("space", "atoms", None, None),
        P("atoms", "space", None),
        P(),
        P("atoms", "space", None, None, None),
        P("atoms", "space", None),
        P("atoms", "space", None),
        P("atoms", "space", None),
        P("atoms", "space", None, None),
    )

    return jax.shard_map(
        per_device,
        mesh=mesh,
        in_specs=placed,
        out_specs=(
            P("atoms", "space", None, None),
            P("atoms", "space", None),
            P("atoms", "space", None, None),
        ),
        check_vma=False,
    )
```

```python
import functools
import math

import jax
import jax.numpy as jnp
from jax import lax
from jax.experimental import pallas as pl
from jax.experimental.pallas import tpu as pltpu
from jax.sharding import PartitionSpec as P

KB = 6


slater_factor = math.pow(3.0 / math.pi, 1.0 / 3.0)
density_floor = 0.05

VMEM = pl.BlockSpec(memory_space=pltpu.VMEM)
SMEM = pl.BlockSpec(memory_space=pltpu.SMEM)


def earlier_count(labels):
    order = jnp.arange(labels.shape[0])
    earlier = (labels[None, :] == labels[:, None]) & (order[None, :] < order[:, None])
    return jnp.sum(earlier.astype(jnp.int32), axis=1)


def requested_blocks(stored, source):
    held_count, block_width, _ = stored.shape
    atom_devices = lax.axis_size("atoms")
    capacity = pl.cdiv(source.shape[0], atom_devices)
    peer_index = source // held_count
    local_index = source % held_count
    slot_index = peer_index * capacity + earlier_count(peer_index)
    wanted = jnp.full((atom_devices * capacity,), -1, jnp.int32).at[slot_index].set(local_index)
    requested = lax.all_to_all(
        wanted.reshape(atom_devices, capacity), "atoms", split_axis=0, concat_axis=0, tiled=True
    )
    flat_request = requested.reshape(-1)
    chosen = jnp.take(stored, jnp.clip(flat_request, 0, held_count - 1), axis=0)
    arrived = lax.all_to_all(
        chosen.reshape(atom_devices, capacity, block_width, block_width),
        "atoms",
        split_axis=0,
        concat_axis=0,
        tiled=True,
    )
    return arrived.reshape(atom_devices * capacity, block_width, block_width), slot_index


upper_tiles = [(i, j) for i in range(KB) for j in range(i, KB)]


def gather_order(devices):
    return sorted(range(1, devices), key=lambda r: (r.bit_count(), -r))


def gathered_blocks(stored):
    devices = lax.axis_size("atoms")
    parts = [stored] + [None] * (devices - 1)
    for offset in gather_order(devices):
        step = 2 if offset == 3 else offset & -offset
        pairs = [(i, i ^ step) for i in range(devices)]
        parts[offset] = lax.ppermute(parts[offset ^ step], "atoms", pairs)
    return jnp.concatenate(parts, axis=0)


def partner(me, step, devices):
    if devices & (devices - 1) == 0:
        return me ^ abs(step)
    return (me + step) % devices


def step_to(me, other, devices):
    if devices & (devices - 1) == 0:
        return me ^ other
    return lax.rem(other - me + devices, devices)


def step_from(me, other, devices):
    if devices & (devices - 1) == 0:
        return me ^ other
    return lax.rem(me - other + devices, devices)


def exchange(groups, sign):
    devices = lax.axis_size("space")
    got = {}
    for step in sorted(groups, reverse=True):
        pairs = [(i, partner(i, sign * step, devices)) for i in range(devices)]
        got[step] = lax.ppermute(groups[step], "space", pairs) if step else groups[step]
    return got


def index_kernel(
    devices, capacity, held, slots, sends, table_ref, atom_ref, me_ref, chem_ref, row_ref, level_ref
):
    me = me_ref[0]
    table = table_ref[...]
    values = []
    for j in range(slots):
        place = table[0, j]
        if held:
            place = (atom_ref[0] ^ lax.div(place, held)) * held + lax.rem(place, held)
        values.append(place)
    dests = [table[0, slots + j] for j in range(sends)]
    for j, dest in enumerate(dests):
        rank = jnp.int32(0)
        for earlier in dests[:j]:
            rank += jnp.where(earlier == dest, 1, 0)
        values.append(step_to(me, dest, devices) * capacity + rank)
    for k in range(devices):
        owner = step_from(me, k, devices)
        for c in range(capacity):
            for side in range(2):
                at = slots + sends + side * devices * capacity
                value = table[0, at]
                for slot in range(1, devices * capacity):
                    value = jnp.where(owner * capacity + c == slot, table[0, at + slot], value)
                values.append(value)
    lanes = lax.broadcasted_iota(jnp.int32, row_ref.shape, 1)
    row = jnp.zeros(row_ref.shape, jnp.int32)
    for j, value in enumerate(values):
        row = jnp.where(lanes == j, value, row)
    row_ref[...] = row
    level_ref[...] = jnp.full(level_ref.shape, chem_ref[0], jnp.float32)


def pair_places(row, sends):
    return [row[0, KB * KB + j] for j in range(sends)]


def sign_kernel(devices, capacity, row_ref, level_ref, block_ref, density_ref, *rest):
    out_refs = rest[:devices]
    x_zero, t_one, x_one, pairs = rest[devices:]
    width = block_ref.shape[-1]
    order = KB * width
    rows = lax.broadcasted_iota(jnp.int32, (width, width), 0)
    cols = lax.broadcasted_iota(jnp.int32, (width, width), 1)
    unit = jnp.where(rows == cols, 1.0, 0.0)
    level = level_ref[...] * unit
    row = row_ref[...]

    def at(i):
        return pl.ds(i * width, width)

    total = jnp.zeros((8, width), jnp.float32)
    shifted = []
    for i, j in upper_tiles:
        upper = block_ref[row[0, i * KB + j]].astype(jnp.float32)
        lower = block_ref[row[0, j * KB + i]].astype(jnp.float32)
        value = 0.5 * (upper + lower.T)
        if i == j:
            value = value - level
        squares = (value * value).reshape(width // 8, 8, width).sum(axis=0)
        total = total + (squares if i == j else 2.0 * squares)
        shifted.append((i, j, value.astype(jnp.bfloat16)))
    for i, j, value in shifted:
        x_zero[at(i), at(j)] = value
        if i != j:
            x_zero[at(j), at(i)] = value.T
    mean = jnp.sum(total, keepdims=True) / order + 1e-06
    inverse = 1.0 / (2.0 * jnp.sqrt(mean))
    weight = -0.5 / (4.0 * mean)
    for i in range(0, KB, 2):
        pair = pl.ds(i * width, 2 * width)
        right = pl.ds(i * width, order - i * width)
        square = jnp.dot(x_zero[pair, :], x_zero[:, right], preferred_element_type=jnp.float32)
        for k in (i, i + 1):
            for j in range(i, KB):
                rows, cols = (k - i) * width, (j - i) * width
                part = weight * square[rows : rows + width, cols : cols + width]
                value = (1.5 * unit + part if k == j else part).astype(jnp.bfloat16)
                t_one[at(k), at(j)] = value
                if j > i + 1:
                    t_one[at(j), at(k)] = value.T
    for i in range(0, KB, 2):
        pair = pl.ds(i * width, 2 * width)
        right = pl.ds(i * width, order - i * width)
        value = jnp.dot(x_zero[pair, :], t_one[:, right], preferred_element_type=jnp.float32)
        value = (inverse * value).astype(jnp.bfloat16)
        x_one[pair, right] = value
        if i + 2 < KB:
            below = pl.ds((i + 2) * width, order - (i + 2) * width)
            x_one[below, pair] = value[:, 2 * width :].T
    square = jnp.dot(x_one[...], x_one[:, at(0)], preferred_element_type=jnp.float32)
    parts = []
    for i in range(KB):
        part = -0.5 * square[i * width : (i + 1) * width]
        parts.append((1.5 * unit + part if i == 0 else part).astype(jnp.bfloat16))
    t_two = jnp.concatenate(parts, axis=0)
    final = jnp.dot(x_one[...], t_two, preferred_element_type=jnp.float32)
    column = []
    for i in range(KB):
        part = final[i * width : (i + 1) * width]
        column.append((0.5 * (unit - part if i == 0 else -part)).astype(jnp.bfloat16))
    for j, place in enumerate(pair_places(row, 2 * KB)):
        pairs[place] = column[j // 2]
    density_ref[...] = jnp.concatenate(column, axis=0)
    for k in range(devices):
        out_refs[k][...] = pairs[k * capacity : (k + 1) * capacity]


def tile_slots(row, steps, capacity):
    slots = []
    for k in steps:
        for c in range(capacity):
            at = KB * KB + 2 * KB + 2 * (k * capacity + c)
            slots.append((k, c, row[0, at], row[0, at + 1]))
    return slots


def pair_density(slots, total, full, table_ref, group_refs):
    width, points = table_ref.shape[1:]
    for k, c, u, v in slots:
        left = table_ref[jnp.maximum(u, 0)].astype(jnp.float32)
        right = table_ref[jnp.maximum(v, 0)]
        product = jnp.dot(group_refs[k][c], right, preferred_element_type=jnp.float32)
        term = (left * product).reshape(width // 8, 8, points).sum(axis=0)
        total = total + term if full else jnp.where(u >= 0, total + term, total)
    return total


def pair_partials(slots, scaled, table_ref, group_refs):
    for k, c, u, v in slots:
        left = table_ref[jnp.maximum(u, 0)].astype(jnp.float32)
        right = table_ref[jnp.maximum(v, 0)]
        weighted = (left * scaled).astype(jnp.bfloat16)
        group_refs[k][c] = lax.dot_general(
            weighted, right, (((1,), (1,)), ((), ())), preferred_element_type=jnp.float32
        ).astype(jnp.bfloat16)


def near_density_kernel(
    capacity, full, steps, row_ref, table_ref, column_ref, *rest
):
    groups = dict(zip(steps, rest[: len(steps)]))
    total_ref, density_ref = rest[len(steps) :]
    density_ref[...] = column_ref[...]
    slots = tile_slots(row_ref[...], steps, capacity)
    total = jnp.zeros(total_ref.shape, jnp.float32)
    total_ref[...] = pair_density(slots, total, full, table_ref, groups)


def mid_density_kernel(capacity, full, steps, row_ref, table_ref, near_ref, *rest):
    groups = dict(zip(steps, rest))
    slots = tile_slots(row_ref[...], steps, capacity)
    rest[-1][...] = pair_density(slots, near_ref[...], full, table_ref, groups)


def partials_kernel(capacity, steps, row_ref, table_ref, weight_ref, found_ref, *rest):
    slots = tile_slots(row_ref[...], steps, capacity)
    pair_partials(slots, weight_ref[...] * found_ref[...], table_ref, dict(zip(steps, rest)))


def last_kernel(
    capacity, full, steps, out_steps, row_ref, table_ref, core_ref, weight_ref, near_ref, *rest
):
    groups = dict(zip(steps, rest[: len(steps)]))
    potential_ref = rest[len(steps)]
    out_groups = dict(zip(out_steps, rest[len(steps) + 1 :]))
    slots = tile_slots(row_ref[...], steps, capacity)
    out_slots = tile_slots(row_ref[...], out_steps, capacity)
    total = pair_density(slots, near_ref[...], full, table_ref, groups)
    valence = jnp.sum(total, axis=0, keepdims=True)
    value = jnp.maximum(core_ref[...] + valence, density_floor)
    root = jnp.exp(jnp.log(value) * (1.0 / 3.0))
    root = root - (root * root * root - value) / (3.0 * root * root)
    potential = -slater_factor * root
    potential_ref[...] = potential
    pair_partials(out_slots, weight_ref[...] * potential, table_ref, out_groups)


def near_partials_kernel(
    capacity, steps, row_ref, table_ref, weight_ref, found_ref, *rest
):
    out_groups = dict(zip(steps, rest))
    potential_ref = rest[len(steps)]
    potential_ref[...] = found_ref[...]
    slots = tile_slots(row_ref[...], steps, capacity)
    pair_partials(slots, weight_ref[...] * found_ref[...], table_ref, out_groups)


def sum_kernel(devices, capacity, row_ref, *rest):
    in_refs = rest[:devices]
    kohn_ref, pairs = rest[devices:]
    width = kohn_ref.shape[-1]
    for k in range(devices):
        pairs[k * capacity : (k + 1) * capacity] = in_refs[k][...]
    places = pair_places(row_ref[...], 2 * KB)
    for i in range(KB):
        kohn_ref[pl.ds(i * width, width), :] = pairs[places[2 * i]].astype(jnp.float32) + pairs[
            places[2 * i + 1]
        ].astype(jnp.float32)


def gathers(slot_count, devices, held_count):
    return devices & (devices - 1) == 0 and pl.cdiv(slot_count, devices) >= held_count


def per_device(
    block_store,
    block_source,
    chem_pot,
    basis_values,
    core_density,
    point_weights,
    pair_dest,
    tile_pairs,
):
    stored = block_store[0]
    held_count, block_width, _ = stored.shape
    source = block_source[0, 0]
    atom_devices = lax.axis_size("atoms")
    devices = lax.axis_size("space")
    destinations = pair_dest[0, 0]
    send_count = destinations.shape[0]
    capacity = pl.cdiv(send_count, devices)
    order = KB * block_width
    direct = gathers(source.shape[0], atom_devices, held_count)
    if direct:
        blocks = gathered_blocks(stored)
    else:
        blocks, source = requested_blocks(stored, source)
    length = source.shape[0] + send_count + 2 * devices * capacity
    length = pl.cdiv(length, 128) * 128
    table = jnp.concatenate([source, destinations, tile_pairs[0, 0].reshape(-1)])
    table = jnp.pad(table, (0, length - table.shape[0])).reshape(1, length)
    row, level = pl.pallas_call(
        functools.partial(
            index_kernel,
            devices,
            capacity,
            held_count if direct else 0,
            source.shape[0],
            send_count,
        ),
        name="index",
        in_specs=[VMEM] + [SMEM] * 3,
        out_shape=[
            jax.ShapeDtypeStruct((1, length), jnp.int32),
            jax.ShapeDtypeStruct((1, block_width), jnp.float32),
        ],
        out_specs=[VMEM] * 2,
        compiler_params=pltpu.CompilerParams(vmem_limit_bytes=1 << 20),
        cost_estimate=pl.CostEstimate(flops=2000, bytes_accessed=2000, transcendentals=0),
    )(
        table,
        lax.axis_index("atoms").reshape(1),
        lax.axis_index("space").reshape(1),
        chem_pot,
    )
    group = jax.ShapeDtypeStruct((capacity, block_width, block_width), jnp.bfloat16)
    out = pl.pallas_call(
        functools.partial(sign_kernel, devices, capacity),
        name="sign",
        in_specs=[VMEM] * 3,
        out_shape=[jax.ShapeDtypeStruct((order, block_width), jnp.bfloat16)] + [group] * devices,
        out_specs=[VMEM] * (1 + devices),
        scratch_shapes=[
            pltpu.VMEM((order, order), jnp.bfloat16),
            pltpu.VMEM((order, order), jnp.bfloat16),
            pltpu.VMEM((order, order), jnp.bfloat16),
            pltpu.VMEM((devices * capacity, block_width, block_width), jnp.bfloat16),
        ],
        compiler_params=pltpu.CompilerParams(vmem_limit_bytes=16 << 20),
        cost_estimate=pl.CostEstimate(
            flops=4 * order**3, bytes_accessed=4 * order * order, transcendentals=0
        ),
    )(row, level, blocks)
    column = out[0]
    outgoing = dict(enumerate(out[1:]))
    near, mid, last = range(2), range(2, devices - 1), range(devices - 1, devices)
    incoming = exchange(outgoing, 1)
    tables = basis_values[0, 0]
    points = tables.shape[-1]
    full = devices * capacity == send_count
    line = jax.ShapeDtypeStruct((1, points), jnp.float32)
    lines = jax.ShapeDtypeStruct((8, points), jnp.float32)

    def step_call(kernel, steps, out_shape, operands):
        pairs = len(steps) * capacity
        return pl.pallas_call(
            kernel,
            in_specs=[VMEM] * len(operands),
            out_shape=out_shape,
            out_specs=[VMEM] * len(out_shape),
            compiler_params=pltpu.CompilerParams(vmem_limit_bytes=16 << 20),
            cost_estimate=pl.CostEstimate(
                flops=2 * pairs * block_width**2 * points,
                bytes_accessed=4 * pairs * block_width * points,
                transcendentals=0,
            ),
        )(*operands)

    total, density = step_call(
        functools.partial(near_density_kernel, capacity, full, near),
        near,
        [lines, column],
        [row, tables, column, *[incoming[k] for k in near]],
    )
    (total,) = step_call(
        functools.partial(mid_density_kernel, capacity, full, mid),
        mid,
        [lines],
        [row, tables, total, *[incoming[k] for k in mid]],
    )
    weight = point_weights[0]
    found, *sent = step_call(
        functools.partial(last_kernel, capacity, full, last, mid),
        last,
        [line] + [group] * len(mid),
        [row, tables, core_density[0], weight, total, *[incoming[k] for k in last]],
    )
    partials = dict(zip(mid, sent))
    sent = step_call(
        functools.partial(partials_kernel, capacity, last),
        last,
        [group] * len(last),
        [row, tables, weight, found],
    )
    partials.update(zip(last, sent))
    *sent, potential = step_call(
        functools.partial(near_partials_kernel, capacity, near),
        near,
        [group] * len(near) + [line],
        [row, tables, weight, found],
    )
    partials.update(zip(near, sent))
    returned = exchange(partials, -1)
    kohn = pl.pallas_call(
        functools.partial(sum_kernel, devices, capacity),
        name="sum",
        in_specs=[VMEM] * (1 + devices),
        out_shape=jax.ShapeDtypeStruct((order, block_width), jnp.float32),
        out_specs=VMEM,
        scratch_shapes=[
            pltpu.VMEM((devices * capacity, block_width, block_width), jnp.bfloat16),
        ],
        compiler_params=pltpu.CompilerParams(vmem_limit_bytes=8 << 20),
    )(row, *[returned[k] for k in range(devices)])
    return (density[None, None], potential[None], kohn[None, None])


def solution(mesh):
    placed = (
        P("space", "atoms", None, None),
        P("atoms", "space", None),
        P(),
        P("atoms", "space", None, None, None),
        P("atoms", "space", None),
        P("atoms", "space", None),
        P("atoms", "space", None),
        P("atoms", "space", None, None),
    )

    return jax.shard_map(
        per_device,
        mesh=mesh,
        in_specs=placed,
        out_specs=(
            P("atoms", "space", None, None),
            P("atoms", "space", None),
            P("atoms", "space", None, None),
        ),
        check_vma=False,
    )
```

```python
import functools
import math

import jax
import jax.numpy as jnp
from jax import lax
from jax.experimental import pallas as pl
from jax.experimental.pallas import tpu as pltpu
from jax.sharding import PartitionSpec as P

KB = 6


slater_factor = math.pow(3.0 / math.pi, 1.0 / 3.0)
density_floor = 0.05

VMEM = pl.BlockSpec(memory_space=pltpu.VMEM)
SMEM = pl.BlockSpec(memory_space=pltpu.SMEM)


def earlier_count(labels):
    order = jnp.arange(labels.shape[0])
    earlier = (labels[None, :] == labels[:, None]) & (order[None, :] < order[:, None])
    return jnp.sum(earlier.astype(jnp.int32), axis=1)


def requested_blocks(stored, source):
    held_count, block_width, _ = stored.shape
    atom_devices = lax.axis_size("atoms")
    capacity = pl.cdiv(source.shape[0], atom_devices)
    peer_index = source // held_count
    local_index = source % held_count
    slot_index = peer_index * capacity + earlier_count(peer_index)
    wanted = jnp.full((atom_devices * capacity,), -1, jnp.int32).at[slot_index].set(local_index)
    requested = lax.all_to_all(
        wanted.reshape(atom_devices, capacity), "atoms", split_axis=0, concat_axis=0, tiled=True
    )
    flat_request = requested.reshape(-1)
    chosen = jnp.take(stored, jnp.clip(flat_request, 0, held_count - 1), axis=0)
    arrived = lax.all_to_all(
        chosen.reshape(atom_devices, capacity, block_width, block_width),
        "atoms",
        split_axis=0,
        concat_axis=0,
        tiled=True,
    )
    return arrived.reshape(atom_devices * capacity, block_width, block_width), slot_index


upper_tiles = [(i, j) for i in range(KB) for j in range(i, KB)]


def gather_order(devices):
    return sorted(range(1, devices), key=lambda r: (r.bit_count(), -r))


def gathered_blocks(stored):
    devices = lax.axis_size("atoms")
    parts = [stored] + [None] * (devices - 1)
    for offset in gather_order(devices):
        step = 2 if offset == 3 else offset & -offset
        pairs = [(i, i ^ step) for i in range(devices)]
        parts[offset] = lax.ppermute(parts[offset ^ step], "atoms", pairs)
    return jnp.concatenate(parts, axis=0)


def partner(me, step, devices):
    if devices & (devices - 1) == 0:
        return me ^ abs(step)
    return (me + step) % devices


def step_to(me, other, devices):
    if devices & (devices - 1) == 0:
        return me ^ other
    return lax.rem(other - me + devices, devices)


def step_from(me, other, devices):
    if devices & (devices - 1) == 0:
        return me ^ other
    return lax.rem(me - other + devices, devices)


def exchange(groups, sign):
    devices = lax.axis_size("space")
    got = {}
    for step in sorted(groups, reverse=True):
        pairs = [(i, partner(i, sign * step, devices)) for i in range(devices)]
        got[step] = lax.ppermute(groups[step], "space", pairs) if step else groups[step]
    return got


def index_kernel(
    devices, capacity, held, slots, sends, table_ref, atom_ref, me_ref, chem_ref, row_ref, level_ref
):
    me = me_ref[0]
    table = table_ref[...]
    values = []
    for j in range(slots):
        place = table[0, j]
        if held:
            place = (atom_ref[0] ^ lax.div(place, held)) * held + lax.rem(place, held)
        values.append(place)
    dests = [table[0, slots + j] for j in range(sends)]
    for j, dest in enumerate(dests):
        rank = jnp.int32(0)
        for earlier in dests[:j]:
            rank += jnp.where(earlier == dest, 1, 0)
        values.append(step_to(me, dest, devices) * capacity + rank)
    for k in range(devices):
        owner = step_from(me, k, devices)
        for c in range(capacity):
            for side in range(2):
                at = slots + sends + side * devices * capacity
                value = table[0, at]
                for slot in range(1, devices * capacity):
                    value = jnp.where(owner * capacity + c == slot, table[0, at + slot], value)
                values.append(value)
    lanes = lax.broadcasted_iota(jnp.int32, row_ref.shape, 1)
    row = jnp.zeros(row_ref.shape, jnp.int32)
    for j, value in enumerate(values):
        row = jnp.where(lanes == j, value, row)
    row_ref[...] = row
    level_ref[...] = jnp.full(level_ref.shape, chem_ref[0], jnp.float32)


def pair_places(row, sends):
    return [row[0, KB * KB + j] for j in range(sends)]


def sign_kernel(devices, capacity, row_ref, level_ref, block_ref, density_ref, *rest):
    out_refs = rest[:devices]
    x_zero, t_one, x_one, pairs = rest[devices:]
    width = block_ref.shape[-1]
    order = KB * width
    rows = lax.broadcasted_iota(jnp.int32, (width, width), 0)
    cols = lax.broadcasted_iota(jnp.int32, (width, width), 1)
    unit = jnp.where(rows == cols, 1.0, 0.0)
    level = level_ref[...] * unit
    row = row_ref[...]

    def at(i):
        return pl.ds(i * width, width)

    total = jnp.zeros((8, width), jnp.float32)
    shifted = []
    for i, j in upper_tiles:
        upper = block_ref[row[0, i * KB + j]].astype(jnp.float32)
        lower = block_ref[row[0, j * KB + i]].astype(jnp.float32)
        value = 0.5 * (upper + lower.T)
        if i == j:
            value = value - level
        squares = (value * value).reshape(width // 8, 8, width).sum(axis=0)
        total = total + (squares if i == j else 2.0 * squares)
        shifted.append((i, j, value))
    mean = jnp.sum(total, keepdims=True) / order + 1e-06
    inverse = 1.0 / (2.0 * jnp.sqrt(mean))
    for i, j, value in shifted:
        value = (value * inverse).astype(jnp.bfloat16)
        x_zero[at(i), at(j)] = value
        if i != j:
            x_zero[at(j), at(i)] = value.T
    for i in range(0, KB, 2):
        pair = pl.ds(i * width, 2 * width)
        right = pl.ds(i * width, order - i * width)
        square = jnp.dot(x_zero[pair, :], x_zero[:, right], preferred_element_type=jnp.float32)
        for k in (i, i + 1):
            for j in range(i, KB):
                rows, cols = (k - i) * width, (j - i) * width
                part = -0.5 * square[rows : rows + width, cols : cols + width]
                value = (1.5 * unit + part if k == j else part).astype(jnp.bfloat16)
                t_one[at(k), at(j)] = value
                if j > i + 1:
                    t_one[at(j), at(k)] = value.T
    for i in range(0, KB, 2):
        pair = pl.ds(i * width, 2 * width)
        right = pl.ds(i * width, order - i * width)
        value = jnp.dot(x_zero[pair, :], t_one[:, right], preferred_element_type=jnp.float32)
        value = value.astype(jnp.bfloat16)
        x_one[pair, right] = value
        if i + 2 < KB:
            below = pl.ds((i + 2) * width, order - (i + 2) * width)
            x_one[below, pair] = value[:, 2 * width :].T
    square = jnp.dot(x_one[at(0), :], x_one[...], preferred_element_type=jnp.float32)
    parts = []
    for i in range(KB):
        part = -0.5 * square[:, i * width : (i + 1) * width]
        parts.append((1.5 * unit + part if i == 0 else part).astype(jnp.bfloat16))
    t_two = jnp.concatenate(parts, axis=1)
    final = jnp.dot(t_two, x_one[...], preferred_element_type=jnp.float32)
    column = []
    for i in range(KB):
        part = final[:, i * width : (i + 1) * width]
        column.append((0.5 * (unit - part if i == 0 else -part)).astype(jnp.bfloat16).T)
    for j, place in enumerate(pair_places(row, 2 * KB)):
        pairs[place] = column[j // 2]
    density_ref[...] = jnp.concatenate(column, axis=0)
    for k in range(devices):
        out_refs[k][...] = pairs[k * capacity : (k + 1) * capacity]


def tile_slots(row, steps, capacity):
    slots = []
    for k in steps:
        for c in range(capacity):
            at = KB * KB + 2 * KB + 2 * (k * capacity + c)
            slots.append((k, c, row[0, at], row[0, at + 1]))
    return slots


def pair_density(slots, total, full, table_ref, group_refs):
    width, points = table_ref.shape[1:]
    for k, c, u, v in slots:
        left = table_ref[jnp.maximum(u, 0)].astype(jnp.float32)
        right = table_ref[jnp.maximum(v, 0)]
        product = jnp.dot(group_refs[k][c], right, preferred_element_type=jnp.float32)
        term = (left * product).reshape(width // 8, 8, points).sum(axis=0)
        total = total + term if full else jnp.where(u >= 0, total + term, total)
    return total


def pair_partials(slots, scaled, table_ref, group_refs):
    for k, c, u, v in slots:
        left = table_ref[jnp.maximum(u, 0)].astype(jnp.float32)
        right = table_ref[jnp.maximum(v, 0)]
        weighted = (left * scaled).astype(jnp.bfloat16)
        group_refs[k][c] = lax.dot_general(
            weighted, right, (((1,), (1,)), ((), ())), preferred_element_type=jnp.float32
        ).astype(jnp.bfloat16)


def near_density_kernel(
    capacity, full, steps, row_ref, table_ref, column_ref, *rest
):
    groups = dict(zip(steps, rest[: len(steps)]))
    total_ref, density_ref = rest[len(steps) :]
    density_ref[...] = column_ref[...]
    slots = tile_slots(row_ref[...], steps, capacity)
    total = jnp.zeros(total_ref.shape, jnp.float32)
    total_ref[...] = pair_density(slots, total, full, table_ref, groups)


def mid_density_kernel(capacity, full, steps, row_ref, table_ref, near_ref, *rest):
    groups = dict(zip(steps, rest))
    slots = tile_slots(row_ref[...], steps, capacity)
    rest[-1][...] = pair_density(slots, near_ref[...], full, table_ref, groups)


def last_kernel(
    capacity, full, steps, out_steps, row_ref, table_ref, core_ref, weight_ref, near_ref, *rest
):
    groups = dict(zip(steps, rest[: len(steps)]))
    potential_ref = rest[len(steps)]
    out_groups = dict(zip(out_steps, rest[len(steps) + 1 :]))
    slots = tile_slots(row_ref[...], steps, capacity)
    out_slots = tile_slots(row_ref[...], out_steps, capacity)
    total = pair_density(slots, near_ref[...], full, table_ref, groups)
    valence = jnp.sum(total, axis=0, keepdims=True)
    value = jnp.maximum(core_ref[...] + valence, density_floor)
    root = jnp.exp(jnp.log(value) * (1.0 / 3.0))
    root = root - (root * root * root - value) / (3.0 * root * root)
    potential = -slater_factor * root
    potential_ref[...] = potential
    pair_partials(out_slots, weight_ref[...] * potential, table_ref, out_groups)


def near_partials_kernel(
    capacity, steps, row_ref, table_ref, weight_ref, found_ref, *rest
):
    out_groups = dict(zip(steps, rest))
    potential_ref = rest[len(steps)]
    potential_ref[...] = found_ref[...]
    slots = tile_slots(row_ref[...], steps, capacity)
    pair_partials(slots, weight_ref[...] * found_ref[...], table_ref, out_groups)


def sum_kernel(devices, capacity, row_ref, *rest):
    in_refs = rest[:devices]
    kohn_ref, pairs = rest[devices:]
    width = kohn_ref.shape[-1]
    for k in range(devices):
        pairs[k * capacity : (k + 1) * capacity] = in_refs[k][...]
    places = pair_places(row_ref[...], 2 * KB)
    for i in range(KB):
        kohn_ref[pl.ds(i * width, width), :] = pairs[places[2 * i]].astype(jnp.float32) + pairs[
            places[2 * i + 1]
        ].astype(jnp.float32)


def gathers(slot_count, devices, held_count):
    return devices & (devices - 1) == 0 and pl.cdiv(slot_count, devices) >= held_count


def per_device(
    block_store,
    block_source,
    chem_pot,
    basis_values,
    core_density,
    point_weights,
    pair_dest,
    tile_pairs,
):
    stored = block_store[0]
    held_count, block_width, _ = stored.shape
    source = block_source[0, 0]
    atom_devices = lax.axis_size("atoms")
    devices = lax.axis_size("space")
    destinations = pair_dest[0, 0]
    send_count = destinations.shape[0]
    capacity = pl.cdiv(send_count, devices)
    order = KB * block_width
    direct = gathers(source.shape[0], atom_devices, held_count)
    if direct:
        blocks = gathered_blocks(stored)
    else:
        blocks, source = requested_blocks(stored, source)
    length = source.shape[0] + send_count + 2 * devices * capacity
    length = pl.cdiv(length, 128) * 128
    table = jnp.concatenate([source, destinations, tile_pairs[0, 0].reshape(-1)])
    table = jnp.pad(table, (0, length - table.shape[0])).reshape(1, length)
    row, level = pl.pallas_call(
        functools.partial(
            index_kernel,
            devices,
            capacity,
            held_count if direct else 0,
            source.shape[0],
            send_count,
        ),
        name="index",
        in_specs=[VMEM] + [SMEM] * 3,
        out_shape=[
            jax.ShapeDtypeStruct((1, length), jnp.int32),
            jax.ShapeDtypeStruct((1, block_width), jnp.float32),
        ],
        out_specs=[VMEM] * 2,
        compiler_params=pltpu.CompilerParams(vmem_limit_bytes=1 << 20),
        cost_estimate=pl.CostEstimate(flops=2000, bytes_accessed=2000, transcendentals=0),
    )(
        table,
        lax.axis_index("atoms").reshape(1),
        lax.axis_index("space").reshape(1),
        chem_pot,
    )
    group = jax.ShapeDtypeStruct((capacity, block_width, block_width), jnp.bfloat16)
    out = pl.pallas_call(
        functools.partial(sign_kernel, devices, capacity),
        name="sign",
        in_specs=[VMEM] * 3,
        out_shape=[jax.ShapeDtypeStruct((order, block_width), jnp.bfloat16)] + [group] * devices,
        out_specs=[VMEM] * (1 + devices),
        scratch_shapes=[
            pltpu.VMEM((order, order), jnp.bfloat16),
            pltpu.VMEM((order, order), jnp.bfloat16),
            pltpu.VMEM((order, order), jnp.bfloat16),
            pltpu.VMEM((devices * capacity, block_width, block_width), jnp.bfloat16),
        ],
        compiler_params=pltpu.CompilerParams(vmem_limit_bytes=16 << 20),
        cost_estimate=pl.CostEstimate(
            flops=4 * order**3, bytes_accessed=4 * order * order, transcendentals=0
        ),
    )(row, level, blocks)
    column = out[0]
    outgoing = dict(enumerate(out[1:]))
    near, mid, last = range(2), range(2, devices - 1), range(devices - 1, devices)
    incoming = exchange(outgoing, 1)
    tables = basis_values[0, 0]
    points = tables.shape[-1]
    full = devices * capacity == send_count
    line = jax.ShapeDtypeStruct((1, points), jnp.float32)
    lines = jax.ShapeDtypeStruct((8, points), jnp.float32)

    def step_call(kernel, steps, out_shape, operands):
        pairs = len(steps) * capacity
        return pl.pallas_call(
            kernel,
            in_specs=[VMEM] * len(operands),
            out_shape=out_shape,
            out_specs=[VMEM] * len(out_shape),
            compiler_params=pltpu.CompilerParams(vmem_limit_bytes=16 << 20),
            cost_estimate=pl.CostEstimate(
                flops=2 * pairs * block_width**2 * points,
                bytes_accessed=4 * pairs * block_width * points,
                transcendentals=0,
            ),
        )(*operands)

    total, density = step_call(
        functools.partial(near_density_kernel, capacity, full, near),
        near,
        [lines, column],
        [row, tables, column, *[incoming[k] for k in near]],
    )
    (total,) = step_call(
        functools.partial(mid_density_kernel, capacity, full, mid),
        mid,
        [lines],
        [row, tables, total, *[incoming[k] for k in mid]],
    )
    weight = point_weights[0]
    found, *sent = step_call(
        functools.partial(last_kernel, capacity, full, last, [*mid, *last]),
        last,
        [line] + [group] * (devices - 2),
        [row, tables, core_density[0], weight, total, *[incoming[k] for k in last]],
    )
    partials = dict(zip([*mid, *last], sent))
    *sent, potential = step_call(
        functools.partial(near_partials_kernel, capacity, near),
        near,
        [group] * len(near) + [line],
        [row, tables, weight, found],
    )
    partials.update(zip(near, sent))
    returned = exchange(partials, -1)
    kohn = pl.pallas_call(
        functools.partial(sum_kernel, devices, capacity),
        name="sum",
        in_specs=[VMEM] * (1 + devices),
        out_shape=jax.ShapeDtypeStruct((order, block_width), jnp.float32),
        out_specs=VMEM,
        scratch_shapes=[
            pltpu.VMEM((devices * capacity, block_width, block_width), jnp.bfloat16),
        ],
        compiler_params=pltpu.CompilerParams(vmem_limit_bytes=8 << 20),
    )(row, *[returned[k] for k in range(devices)])
    return (density[None, None], potential[None], kohn[None, None])


def solution(mesh):
    placed = (
        P("space", "atoms", None, None),
        P("atoms", "space", None),
        P(),
        P("atoms", "space", None, None, None),
        P("atoms", "space", None),
        P("atoms", "space", None),
        P("atoms", "space", None),
        P("atoms", "space", None, None),
    )

    return jax.shard_map(
        per_device,
        mesh=mesh,
        in_specs=placed,
        out_specs=(
            P("atoms", "space", None, None),
            P("atoms", "space", None),
            P("atoms", "space", None, None),
        ),
        check_vma=False,
    )
```
